256 devices in a mesh: grid: 128 (over y_lo, x, z, core), batch: 2 (over y_hi).
Axes of the slice: x: 4, y: 4 (y_hi: 2, y_lo: 2; y = y_hi * 2 + y_lo), z: 8, core: 2. Of those that a mesh axis runs over, the one named last changes fastest.
Arguments:
- orbitals: bfloat16 [1024, 262144], P(None, 'grid'), may hold values from -0.1875 to 0.1875
- points: int32 [2, 256], P('batch'), may hold values from 0 to 262143, as said below
Outputs:
- kernel: float32 [512, 512], P('batch', 'grid')
The draws below stay inside these ranges and needn't reach their ends.
Inputs may be any that keep to these rules, and one draw needn't show every extreme that they name: `points`: each entry is a cell index (x * 64 + y) * 64 + z.
All inputs are finite; a program needn't handle non-finite values.
Results may differ from the reference program's by a relative error of at most 0.0006.
The reference program's roundings to bfloat16 on the way count: a program that leaves them out, or rounds other values in their place, can miss the bound.
Values may be sent and summed in bfloat16 or wider, within the bound.
No kernel may reach another device: no remote copies, remote signals or barrier semaphores. Data moves between devices by JAX's collectives and lax.ppermute only.
A program may use at most 64 MiB of HBM per device.

```python
import math
import jax
import jax.numpy as jnp
from jax import lax

NX = 64
NY = 64
NZ = 64
NORB = 1024
NFIT = 256
NCELL = 262144
N_BATCH = 2


def draw_points(key, part):
    base = jax.random.fold_in(key, 11)
    key_x, key_y, key_z, key_shift = jax.random.split(base, 4)
    centre_x = jax.random.randint(key_x, (NFIT,), 0, NX)
    centre_y = jax.random.randint(key_y, (NFIT,), 0, NY)
    centre_z = jax.random.randint(key_z, (NFIT,), 0, NZ)
    centre_x = centre_x.at[0].set(NX - 1).at[1].set(0)
    centre_y = centre_y.at[0].set(NY - 1).at[1].set(0)
    centre_z = centre_z.at[0].set(NZ - 1).at[1].set(0)
    shifts = jax.random.randint(key_shift, (N_BATCH, NFIT, 3), -2, 3)
    shifts = shifts.at[0, 0:2].set(0)
    place_x = jnp.remainder(centre_x[None, :] + shifts[:, :, 0], NX)
    place_y = jnp.remainder(centre_y[None, :] + shifts[:, :, 1], NY)
    place_z = jnp.remainder(centre_z[None, :] + shifts[:, :, 2], NZ)
    return ((place_x * NY + place_y) * NZ + place_z).astype(jnp.int32)


def shard_levels(own_key, dims, cuts, low, high):
    def one(position, blocks):
        draws = jax.random.uniform(jax.random.fold_in(jax.random.fold_in(own_key, 6), position), (blocks,), jnp.float32, low / len(cuts), high / len(cuts))
        return jnp.repeat(jnp.exp(draws), dims[position] // blocks).reshape((-1,) + (1,) * (len(dims) - position - 1))

    level = one(*cuts[0])
    for cut in cuts[1:]:
        level = level * one(*cut)
    return level


def centred(own_key, dims, spread, most, pieces=(), kind=jnp.bfloat16):
    drawn = jax.random.normal(own_key, dims, jnp.float32) * spread
    if len(pieces) > 0:
        drawn = shard_levels(own_key, dims, pieces, -0.22, 0.18) * drawn
    return jnp.clip(drawn, min=-most, max=most).astype(kind)


def setup_inputs(seed: int = 0) -> dict:
    splits = jax.random.split(jax.random.key(seed), 3)
    return {
        "orbitals": centred(splits[0], (NORB, NCELL), NORB ** -0.5, 0.1875, ((1, 128),)),
        "points": draw_points(jax.random.fold_in(splits[2], 71), 0),
    }


screen_rate = 0.05
kernel_scale = 16.0

def make_tables(length):
    rows = jnp.arange(length, dtype=jnp.int32)[:, None]
    columns = jnp.arange(length, dtype=jnp.int32)[None, :]
    angles = (rows * columns % length).astype(jnp.float32) * jnp.float32(2.0 * math.pi / length)
    cosine = (jnp.cos(angles) / math.sqrt(length)).astype(jnp.bfloat16)
    sine = (jnp.sin(angles) / math.sqrt(length)).astype(jnp.bfloat16)
    return (cosine, sine)

def signed_freq(values, length):
    return jnp.where(values < length // 2, values, values - length).astype(jnp.float32)

def screen_weights(z_modes):
    mode_z = signed_freq(z_modes, NZ)[:, None, None]
    mode_x = signed_freq(jnp.arange(NX, dtype=jnp.int32), NX)[None, :, None]
    mode_y = signed_freq(jnp.arange(NY, dtype=jnp.int32), NY)[None, None, :]
    scaled = screen_rate * (mode_x * mode_x + mode_y * mode_y + mode_z * mode_z)
    positive = scaled > 0
    safe_scaled = jnp.where(positive, scaled, jnp.float32(1.0))
    return jnp.where(positive, -jnp.expm1(-safe_scaled) / safe_scaled, jnp.float32(0.0)).astype(jnp.float32)

def plane_transform(planes):
    count = planes.shape[0]
    items = planes.shape[2]
    cos_y, sin_y = make_tables(NY)
    cos_x, sin_x = make_tables(NX)
    y_table = jnp.stack([cos_y, -sin_y])
    x_table = jnp.concatenate([jnp.concatenate([cos_x, sin_x], 1), jnp.concatenate([-sin_x, cos_x], 1)], 0)
    layout = planes.reshape(count, NX, NY, items)
    half_y = jnp.einsum('dky,cxyp->cdxkp', y_table.astype(jnp.float32), layout.astype(jnp.float32)).astype(jnp.bfloat16)
    flat = half_y.reshape(count, 2 * NX, NY * items)
    spectra = jnp.einsum('ab,cbm->cam', x_table.astype(jnp.float32), flat.astype(jnp.float32)).astype(jnp.bfloat16)
    return spectra.reshape(count, 2, NX, NY, items)

def reference(orbitals, points):
    flat_points = points.reshape(-1).astype(jnp.int32)
    total = flat_points.shape[0]
    point_values = jnp.take(orbitals, flat_points, axis=1)
    block_size = 32
    blocks = total // block_size
    grouped = point_values.reshape(NORB, blocks, block_size).transpose(1, 0, 2)
    cos_z, sin_z = make_tables(NZ)
    z_table = jnp.concatenate([cos_z, -sin_z], 0)
    screen = screen_weights(jnp.arange(NZ, dtype=jnp.int32))

    def block_coeffs(values_block):
        density = jnp.dot(values_block.T, orbitals, preferred_element_type=jnp.float32)
        fitted = (density * density).astype(jnp.bfloat16).reshape(block_size, NX * NY, NZ)
        half_z = jnp.einsum('kz,paz->kap', z_table.astype(jnp.float32), fitted.astype(jnp.float32)).astype(jnp.bfloat16)
        spectra = plane_transform(half_z).reshape(2, NZ, 2, NX, NY, block_size).astype(jnp.float32)
        real_coeff = spectra[0, :, 0] - spectra[1, :, 1]
        imag_coeff = spectra[1, :, 0] + spectra[0, :, 1]
        coeffs = jnp.stack([real_coeff, imag_coeff]).astype(jnp.bfloat16)
        weighted = (coeffs.astype(jnp.float32) * screen[None, :, :, :, None]).astype(jnp.bfloat16)
        return (coeffs, weighted)
    coeffs, weighted = lax.map(block_coeffs, grouped)

    def accumulate(carry, plane):
        coeff_plane = lax.dynamic_index_in_dim(coeffs, plane, 2, keepdims=False)
        weight_plane = lax.dynamic_index_in_dim(weighted, plane, 2, keepdims=False)
        coeff_mat = jnp.moveaxis(coeff_plane, 0, 3).reshape(2 * NX * NY, total)
        weight_mat = jnp.moveaxis(weight_plane, 0, 3).reshape(2 * NX * NY, total)
        return (carry + jnp.dot(weight_mat.T, coeff_mat, preferred_element_type=jnp.float32), None)
    gram, _ = lax.scan(accumulate, jnp.zeros((total, total), jnp.float32), jnp.arange(NZ, dtype=jnp.int32))
    return kernel_scale * gram
```

```python
import math

import jax
import jax.numpy as jnp
from jax import lax
from jax.experimental import pallas as pl
from jax.experimental.pallas import tpu as pltpu
from jax.sharding import Mesh
from jax.sharding import PartitionSpec as P

N = 64
NORB = 1024
NFIT = 256
HALF = NFIT // 2

screen_rate = 0.05
kernel_scale = 16.0

CHIPS = ("yl", "x", "z")
SAME_CORE = ("yl", "x", "z", "b")
F32 = jnp.float32
BF16 = jnp.bfloat16


def signed_freq(values):
    return jnp.where(values < N // 2, values, values - N).astype(F32)


def waves(freq, place):
    angles = (freq * place % N).astype(F32) * F32(2.0 * math.pi / N)
    return jnp.cos(angles) / math.sqrt(N), jnp.sin(angles) / math.sqrt(N)


def iota(shape, dim):
    return lax.broadcasted_iota(jnp.int32, shape, dim)


def pair_table(row, place):
    pair, part = row // 2, row % 2
    freq = jnp.where((pair == 0) & (part == 1), N // 2, pair)
    cosine, sine = waves(freq, place)
    return jnp.where((part == 0) | (pair == 0), cosine, -sine)


def x_table(lone):
    row, column = iota((256, 256), 0), iota((256, 256), 1)
    z_of, e, k = row // 128, row // 64 % 2, row % 64
    z_part, y_part, place = column // 128, column // 64 % 2, column % 64
    k_low = k % 32
    turned = (e == 1) & (k_low == 0)
    freq = jnp.where(lone, jnp.where(turned, N // 2, k_low), k)
    cosine, sine = waves(freq, place)
    both = jnp.where(e == y_part, cosine, jnp.where(e == 0, sine, -sine))
    both = jnp.where(z_of == z_part, both, F32(0.0))
    single = jnp.where((e == 0) | turned, cosine, -sine)
    kept = (y_part == k // 32) & (z_part == jnp.where(turned, 1 - z_of, z_of))
    return jnp.where(lone, jnp.where(kept, single, F32(0.0)), both).astype(BF16)


def screen_rows(y_pair, z_first):
    shape = (1024, 128)
    row = iota(shape, 0)
    out, k, z_pair = row // 256, row // 4 % 64, z_first + row % 4
    lone_y, lone_z = y_pair == 0, z_pair == 0
    k_low = k % 32
    edge = lone_y & (k_low == 0)
    second = (out == 1) | (out == 3)
    kx = jnp.where(lone_y, jnp.where(edge & second, N // 2, k_low), k)
    ky = jnp.where(lone_y, jnp.where(k >= 32, N // 2, 0), y_pair)
    z_late = (out == 2) | jnp.where(edge, out == 3, out == 1)
    kz = jnp.where(lone_z, jnp.where(z_late, N // 2, 0), z_pair)
    fx, fy, fz = signed_freq(kx), signed_freq(ky), signed_freq(kz)
    scaled = screen_rate * (fx * fx + fy * fy + fz * fz)
    positive = scaled > 0
    safe = jnp.where(positive, scaled, F32(1.0))
    screen = jnp.where(positive, -jnp.expm1(-safe) / safe, F32(0.0))
    copies = jnp.where(edge & lone_z, F32(1.0), F32(2.0))
    mixed = jnp.where(lone_z | edge, F32(0.0), F32(1.0))[:256]
    return screen * copies, mixed


def expand_kernel(y_small_ref, x_small_ref, y_ref, x_ref):
    block = pl.program_id(0)
    row = 256 * block + iota((256, 1024), 0)
    column = iota((256, 1024), 1)

    def spread(small, row_of, column_of):
        r = 256 * block + iota((256, small.shape[0]), 0)
        c = iota((small.shape[1], 1024), 1)
        left = jnp.where(row_of(r) == iota(r.shape, 1), F32(1.0), F32(0.0)).astype(BF16)
        right = jnp.where(column_of(c) == iota(c.shape, 0), F32(1.0), F32(0.0)).astype(BF16)
        tall = jnp.dot(left, small, preferred_element_type=F32).astype(BF16)
        return jnp.dot(tall, right, preferred_element_type=F32)

    wide = spread(y_small_ref[...], lambda r: (r >> 5) * 2 + ((r >> 3) & 1), lambda c: c >> 4)
    same = (((row >> 4) & 1) == ((column >> 3) & 1)) & ((row & 7) == (column & 7))
    y_ref[...] = jnp.where(same, wide, F32(0.0)).astype(BF16)
    wide = spread(
        x_small_ref[...],
        lambda r: r >> 2,
        lambda c: (c & 1) * 128 + ((c >> 3) & 1) * 64 + (c >> 4),
    )
    same = (row & 3) == ((column >> 1) & 3)
    x_ref[...] = jnp.where(same, wide, F32(0.0)).astype(BF16)


def expand(y_small, x_small):
    big = jax.ShapeDtypeStruct((1024, 1024), BF16)
    return pl.pallas_call(
        expand_kernel,
        out_shape=(big, big),
        grid=(4,),
        in_specs=[
            pl.BlockSpec((N, N), lambda i: (0, 0)),
            pl.BlockSpec((256, 256), lambda i: (0, 0)),
        ],
        out_specs=[pl.BlockSpec((256, 1024), lambda i: (i, 0))] * 2,
        cost_estimate=pl.CostEstimate(flops=2**31, bytes_accessed=2**22, transcendentals=0),
        name="expand",
    )(y_small, x_small)


def pick_kernel(offsets_ref, orbitals_ref, own_ref, other_ref, hot_ref):
    @pl.when(pl.program_id(0) == 0)
    def _():
        cell = lax.broadcasted_iota(jnp.int32, (2048, NFIT), 0)
        hot_ref[...] = jnp.where(cell == offsets_ref[...], F32(1.0), F32(0.0)).astype(BF16)

    got = jnp.dot(orbitals_ref[...], hot_ref[...], preferred_element_type=F32).astype(BF16)
    own_ref[...] = got[:, :HALF]
    other_ref[...] = got[:, HALF:]


def pick(offsets, orbitals):
    rows = 256
    half = jax.ShapeDtypeStruct((NORB, HALF), BF16)
    return pl.pallas_call(
        pick_kernel,
        out_shape=(half, half),
        grid=(NORB // rows,),
        in_specs=[
            pl.BlockSpec((1, NFIT), lambda i: (0, 0)),
            pl.BlockSpec((rows, 2048), lambda i: (i, 0)),
        ],
        out_specs=[pl.BlockSpec((rows, HALF), lambda i: (i, 0))] * 2,
        scratch_shapes=[pltpu.VMEM((2048, NFIT), BF16)],
        name="pick",
    )(offsets, orbitals)


def fit_kernel(core_ref, own_ref, other_ref, table_ref, orbitals_ref, near_ref, far_ref, values_ref):
    @pl.when(pl.program_id(0) == 0)
    def _():
        core = core_ref[0]
        mine = pl.multiple_of(core * HALF, HALF)
        theirs = pl.multiple_of((1 - core) * HALF, HALF)
        values_ref[pl.ds(mine, HALF), :] = own_ref[...].astype(F32).T.astype(BF16)
        values_ref[pl.ds(theirs, HALF), :] = other_ref[...].astype(F32).T.astype(BF16)

    density = jnp.dot(values_ref[...], orbitals_ref[...], preferred_element_type=F32)
    fitted = (density * density).astype(BF16)
    for s in range(2):
        half_z = lax.dot_general(
            table_ref[...],
            fitted[:, 256 * s : 256 * s + 256],
            (((1,), (1,)), ((), ())),
            preferred_element_type=F32,
        ).astype(BF16)
        near_ref[4 * s : 4 * s + 4] = half_z[:128].reshape(4, 32, NFIT)
        far_ref[4 * s : 4 * s + 4] = half_z[128:].reshape(4, 32, NFIT)


def fit(core, own, other, table, orbitals):
    half = jax.ShapeDtypeStruct((32, 32, NFIT), BF16)
    return pl.pallas_call(
        fit_kernel,
        out_shape=(half, half),
        grid=(4,),
        in_specs=[
            pl.BlockSpec(memory_space=pltpu.SMEM),
            pl.BlockSpec((NORB, HALF), lambda i: (0, 0)),
            pl.BlockSpec((NORB, HALF), lambda i: (0, 0)),
            pl.BlockSpec((256, 256), lambda i: (0, 0)),
            pl.BlockSpec((NORB, 512), lambda i: (0, i)),
        ],
        out_specs=[pl.BlockSpec((8, 32, NFIT), lambda i: (i, 0, 0))] * 2,
        scratch_shapes=[pltpu.VMEM((NFIT, NORB), BF16)],
        name="fit",
    )(core, own, other, table, orbitals)


def y_kernel(core_ref, near_ref, far_ref, table_ref, out_ref, rows_ref):
    core = core_ref[0]
    mine = pl.multiple_of(core * 512, 512)
    theirs = pl.multiple_of((1 - core) * 512, 512)
    for g in range(2):
        rows_ref[pl.ds(mine, 512), :] = near_ref[:, 16 * g : 16 * g + 16, :].reshape(512, NFIT)
        rows_ref[pl.ds(theirs, 512), :] = far_ref[:, 16 * g : 16 * g + 16, :].reshape(512, NFIT)
        for m in range(4):
            got = jnp.dot(
                table_ref[256 * m : 256 * m + 256, :], rows_ref[...], preferred_element_type=F32
            ).astype(BF16)
            out_ref[8 * m : 8 * m + 8, g] = got.reshape(8, 2, 16, NFIT)


def y_transform(core, near, far, table):
    return pl.pallas_call(
        y_kernel,
        out_shape=jax.ShapeDtypeStruct((32, 2, 2, 16, NFIT), BF16),
        in_specs=[pl.BlockSpec(memory_space=pltpu.SMEM)]
        + [pl.BlockSpec(memory_space=pltpu.VMEM)] * 3,
        out_specs=pl.BlockSpec(memory_space=pltpu.VMEM),
        scratch_shapes=[pltpu.VMEM((1024, NFIT), BF16)],
        name="y_transform",
    )(core, near, far, table)


def gram_kernel(
    core_ref, planes_ref, table_ref, screen_ref, mixed_ref, own_ref, other_ref, coeffs_ref, weighted_ref
):
    mixed = jnp.concatenate([mixed_ref[...]] * 2, axis=1)
    for b in range(2):
        rows = planes_ref[:, b].reshape(1024, NFIT)
        t0, t1, t2, t3 = [
            jnp.dot(table_ref[256 * t : 256 * t + 256, :], rows, preferred_element_type=F32)
            .astype(BF16)
            .astype(F32)
            for t in range(4)
        ]
        outs = (t0 - mixed * t3, mixed * t0 + t3, t2 + mixed * t1, mixed * t2 - t1)
        for o, value in enumerate(outs):
            at = slice(256 * o, 256 * o + 256)
            value = value.astype(BF16)
            coeffs_ref[at, 256 * b : 256 * b + 256] = value
            value = value.astype(F32)
            screen = screen_ref[at, :]
            for h in range(2):
                weighted_ref[h, at, 128 * b : 128 * b + 128] = (
                    value[:, 128 * h : 128 * h + 128] * screen
                ).astype(BF16)
    core = core_ref[0]
    for q in range(2):
        left = coeffs_ref[:, 256 * q : 256 * q + 256]
        for half, out_ref in ((core, own_ref), (1 - core, other_ref)):
            got = kernel_scale * lax.dot_general(
                left, weighted_ref[half], (((0,), (0,)), ((), ())), preferred_element_type=F32
            )
            for b in range(2):
                out_ref[32 * q : 32 * q + 32, b] = got[:, 128 * b : 128 * b + 128].reshape(32, 8, 128)


def gram(core, planes, table, screen, mixed):
    half = jax.ShapeDtypeStruct((N, 2, 8, 128), F32)
    return pl.pallas_call(
        gram_kernel,
        out_shape=(half, half),
        in_specs=[pl.BlockSpec(memory_space=pltpu.SMEM)]
        + [pl.BlockSpec(memory_space=pltpu.VMEM)] * 4,
        out_specs=[pl.BlockSpec(memory_space=pltpu.VMEM)] * 2,
        scratch_shapes=[pltpu.VMEM((1024, 512), BF16), pltpu.VMEM((2, 1024, 256), BF16)],
        name="gram",
    )(core, planes, table, screen, mixed)


def sibling(block):
    return lax.ppermute(block, "c", [(0, 1), (1, 0)])


def exchange(blocks, axes):
    return lax.all_to_all(blocks, axes, split_axis=0, concat_axis=0, tiled=True)


def on_device(orbitals, points):
    core = lax.axis_index("c")
    batch = lax.axis_index("b")
    chip = lax.axis_index(CHIPS)
    core_word = core.astype(jnp.int32)[None]
    y_pair, z_group = chip // 2, core * 4 + chip % 2 * 2 + batch
    small = pair_table(iota((N, N), 0), iota((N, N), 1)).astype(BF16)
    z_row, z_column = iota((256, 256), 0), iota((256, 256), 1)
    z_half = jnp.where(z_row < 128, core, 1 - core)
    z_table = pair_table(z_half * 32 + z_row % 32, z_column % N)
    z_table = jnp.where(z_row // 32 % 4 == z_column // N, z_table, F32(0.0)).astype(BF16)
    y_big, x_big = expand(small, x_table(y_pair == 0))
    screen, mixed = screen_rows(y_pair, z_group * 4)

    halves = points[0].reshape(2, HALF)
    halves = jnp.where(core == 0, halves, halves[::-1])
    offsets = halves.reshape(1, NFIT) - (chip * 2 + core) * 2048
    own, other = pick(offsets, orbitals)
    own = exchange((own + sibling(other)).reshape(N, 16, HALF), CHIPS)
    own = jnp.sum(own.astype(F32), axis=0).astype(BF16)
    own = exchange(jnp.broadcast_to(own[None], (N, 16, HALF)), CHIPS).reshape(NORB, HALF)
    other = sibling(own)
    near, far = fit(core_word, own, other, z_table, orbitals)
    planes = y_transform(core_word, near, sibling(far), y_big)
    planes = exchange(planes.reshape(128, 16, NFIT), SAME_CORE).reshape(N, 2, 16, NFIT)
    own, other = gram(core_word, planes, x_big, screen, mixed)
    sums = exchange((own + sibling(other)).reshape(128, 8, 128), SAME_CORE)
    sums = jnp.sum(sums, axis=0).reshape(2, 4, 128)
    mine = lax.dynamic_index_in_dim(sums, core, 0, keepdims=False)
    theirs = sibling(lax.dynamic_index_in_dim(sums, 1 - core, 0, keepdims=False))
    pair = jnp.where(core == 0, jnp.stack([mine, theirs]), jnp.stack([theirs, mine]))
    return pair.transpose(0, 2, 1).reshape(NFIT, 4)


def solution(mesh):
    fine = Mesh(mesh.devices.reshape(2, 4, 8, 2, 2), ("yl", "x", "z", "c", "b"))
    grid = ("yl", "x", "z", "c")
    return jax.shard_map(
        on_device,
        mesh=fine,
        in_specs=(P(None, grid), P("b", None)),
        out_specs=P("b", grid),
        check_vma=False,
    )
```

```python
import math

import jax
import jax.numpy as jnp
from jax import lax
from jax.experimental import pallas as pl
from jax.experimental.pallas import tpu as pltpu
from jax.sharding import Mesh
from jax.sharding import PartitionSpec as P

N = 64
NORB = 1024
NFIT = 256
HALF = NFIT // 2

screen_rate = 0.05
kernel_scale = 16.0

CHIPS = ("yl", "x", "z")
SAME_CORE = ("yl", "x", "z", "b")
F32 = jnp.float32
BF16 = jnp.bfloat16


def signed_freq(values):
    return jnp.where(values < N // 2, values, values - N).astype(F32)


def waves(freq, place):
    angles = (freq * place % N).astype(F32) * F32(2.0 * math.pi / N)
    return jnp.cos(angles) / math.sqrt(N), jnp.sin(angles) / math.sqrt(N)


def iota(shape, dim):
    return lax.broadcasted_iota(jnp.int32, shape, dim)


def pair_table(row, place):
    pair, part = row // 2, row % 2
    freq = jnp.where((pair == 0) & (part == 1), N // 2, pair)
    cosine, sine = waves(freq, place)
    return jnp.where((part == 0) | (pair == 0), cosine, -sine)


def x_table(lone):
    row, column = iota((256, 256), 0), iota((256, 256), 1)
    z_of, e, k = row // 128, row // 64 % 2, row % 64
    z_part, y_part, place = column // 128, column // 64 % 2, column % 64
    k_low = k % 32
    turned = (e == 1) & (k_low == 0)
    freq = jnp.where(lone, jnp.where(turned, N // 2, k_low), k)
    cosine, sine = waves(freq, place)
    both = jnp.where(e == y_part, cosine, jnp.where(e == 0, sine, -sine))
    both = jnp.where(z_of == z_part, both, F32(0.0))
    single = jnp.where((e == 0) | turned, cosine, -sine)
    kept = (y_part == k // 32) & (z_part == jnp.where(turned, 1 - z_of, z_of))
    return jnp.where(lone, jnp.where(kept, single, F32(0.0)), both).astype(BF16)


def screen_rows(y_pair, z_first):
    shape = (1024, 128)
    row = iota(shape, 0)
    out, k, z_pair = row // 256, row // 4 % 64, z_first + row % 4
    lone_y, lone_z = y_pair == 0, z_pair == 0
    k_low = k % 32
    edge = lone_y & (k_low == 0)
    second = (out == 1) | (out == 3)
    kx = jnp.where(lone_y, jnp.where(edge & second, N // 2, k_low), k)
    ky = jnp.where(lone_y, jnp.where(k >= 32, N // 2, 0), y_pair)
    z_late = (out == 2) | jnp.where(edge, out == 3, out == 1)
    kz = jnp.where(lone_z, jnp.where(z_late, N // 2, 0), z_pair)
    fx, fy, fz = signed_freq(kx), signed_freq(ky), signed_freq(kz)
    scaled = screen_rate * (fx * fx + fy * fy + fz * fz)
    positive = scaled > 0
    safe = jnp.where(positive, scaled, F32(1.0))
    screen = jnp.where(positive, -jnp.expm1(-safe) / safe, F32(0.0))
    copies = jnp.where(edge & lone_z, F32(1.0), F32(2.0))
    mixed = jnp.where(lone_z | edge, F32(0.0), F32(1.0))[:256]
    return screen * copies, mixed


def expand_kernel(y_small_ref, x_small_ref, y_ref, x_ref):
    block = pl.program_id(0)
    row = 256 * block + iota((256, 1024), 0)
    column = iota((256, 1024), 1)

    def spread(small, row_of, column_of):
        r = 256 * block + iota((256, small.shape[0]), 0)
        c = iota((small.shape[1], 1024), 1)
        left = jnp.where(row_of(r) == iota(r.shape, 1), F32(1.0), F32(0.0)).astype(BF16)
        right = jnp.where(column_of(c) == iota(c.shape, 0), F32(1.0), F32(0.0)).astype(BF16)
        tall = jnp.dot(left, small, preferred_element_type=F32).astype(BF16)
        return jnp.dot(tall, right, preferred_element_type=F32)

    wide = spread(y_small_ref[...], lambda r: (r >> 5) * 2 + ((r >> 3) & 1), lambda c: c >> 4)
    same = (((row >> 4) & 1) == ((column >> 3) & 1)) & ((row & 7) == (column & 7))
    y_ref[...] = jnp.where(same, wide, F32(0.0)).astype(BF16)
    wide = spread(
        x_small_ref[...],
        lambda r: r >> 2,
        lambda c: (c & 1) * 128 + ((c >> 3) & 1) * 64 + (c >> 4),
    )
    same = (row & 3) == ((column >> 1) & 3)
    x_ref[...] = jnp.where(same, wide, F32(0.0)).astype(BF16)


def expand(y_small, x_small):
    big = jax.ShapeDtypeStruct((1024, 1024), BF16)
    return pl.pallas_call(
        expand_kernel,
        out_shape=(big, big),
        grid=(4,),
        in_specs=[
            pl.BlockSpec((N, N), lambda i: (0, 0)),
            pl.BlockSpec((256, 256), lambda i: (0, 0)),
        ],
        out_specs=[pl.BlockSpec((256, 1024), lambda i: (i, 0))] * 2,
        cost_estimate=pl.CostEstimate(flops=2**31, bytes_accessed=2**22, transcendentals=0),
        compiler_params=pltpu.CompilerParams(vmem_limit_bytes=16 << 20),
        name="expand",
    )(y_small, x_small)


def pick_kernel(offsets_ref, orbitals_ref, own_ref, other_ref, held_ref, hot_ref, sem):
    copy = pltpu.make_async_copy(orbitals_ref, held_ref, sem)
    copy.start()
    cell = iota((2048, NFIT), 0)
    hot_ref[...] = jnp.where(cell == offsets_ref[...], F32(1.0), F32(0.0)).astype(BF16)
    copy.wait()
    got = jnp.dot(held_ref[...], hot_ref[...], preferred_element_type=F32).astype(BF16)
    own_ref[...] = got[:, :HALF]
    other_ref[...] = got[:, HALF:]


def pick(offsets, orbitals):
    half = jax.ShapeDtypeStruct((NORB, HALF), BF16)
    vmem = pl.BlockSpec(memory_space=pltpu.VMEM)
    return pl.pallas_call(
        pick_kernel,
        out_shape=(half, half),
        in_specs=[vmem, pl.BlockSpec(memory_space=pltpu.HBM)],
        out_specs=[vmem] * 2,
        scratch_shapes=[
            pltpu.VMEM((NORB, 2048), BF16),
            pltpu.VMEM((2048, NFIT), BF16),
            pltpu.SemaphoreType.DMA(()),
        ],
        compiler_params=pltpu.CompilerParams(vmem_limit_bytes=16 << 20),
        name="pick",
    )(offsets, orbitals)


def hold_kernel(orbitals_ref, held_ref, sem):
    copy = pltpu.make_async_copy(orbitals_ref, held_ref, sem)
    copy.start()
    copy.wait()


def hold(orbitals):
    return pl.pallas_call(
        hold_kernel,
        out_shape=jax.ShapeDtypeStruct(orbitals.shape, orbitals.dtype),
        in_specs=[pl.BlockSpec(memory_space=pltpu.HBM)],
        out_specs=pl.BlockSpec(memory_space=pltpu.VMEM),
        scratch_shapes=[pltpu.SemaphoreType.DMA(())],
        compiler_params=pltpu.CompilerParams(vmem_limit_bytes=8 << 20),
        cost_estimate=pl.CostEstimate(flops=0, bytes_accessed=2**23, transcendentals=0),
        name="hold",
    )(orbitals)


def fit_kernel(core_ref, own_ref, other_ref, table_ref, orbitals_ref, near_ref, far_ref, values_ref):
    core = core_ref[0]
    mine = pl.multiple_of(core * HALF, HALF)
    theirs = pl.multiple_of((1 - core) * HALF, HALF)
    values_ref[:, pl.ds(mine, HALF)] = own_ref[...]
    values_ref[:, pl.ds(theirs, HALF)] = other_ref[...]
    density = lax.dot_general(
        orbitals_ref[...], values_ref[...], (((0,), (0,)), ((), ())), preferred_element_type=F32
    )
    fitted = (density * density).astype(BF16)
    for j in range(8):
        half_z = jnp.dot(
            table_ref[...], fitted[256 * j : 256 * j + 256], preferred_element_type=F32
        ).astype(BF16)
        near_ref[4 * j : 4 * j + 4] = half_z[:128].reshape(4, 32, NFIT)
        far_ref[4 * j : 4 * j + 4] = half_z[128:].reshape(4, 32, NFIT)


def fit(core, own, other, table, held):
    half = jax.ShapeDtypeStruct((32, 32, NFIT), BF16)
    vmem = pl.BlockSpec(memory_space=pltpu.VMEM)
    return pl.pallas_call(
        fit_kernel,
        out_shape=(half, half),
        in_specs=[pl.BlockSpec(memory_space=pltpu.SMEM)] + [vmem] * 4,
        out_specs=[vmem] * 2,
        scratch_shapes=[pltpu.VMEM((NORB, NFIT), BF16)],
        compiler_params=pltpu.CompilerParams(vmem_limit_bytes=16 << 20),
        name="fit",
    )(core, own, other, table, held)


def y_kernel(core_ref, near_ref, far_ref, table_ref, out_ref, rows_ref):
    core = core_ref[0]
    mine = pl.multiple_of(core * 512, 512)
    theirs = pl.multiple_of((1 - core) * 512, 512)
    for g in range(2):
        rows_ref[pl.ds(mine, 512), :] = near_ref[:, 16 * g : 16 * g + 16, :].reshape(512, NFIT)
        rows_ref[pl.ds(theirs, 512), :] = far_ref[:, 16 * g : 16 * g + 16, :].reshape(512, NFIT)
        for m in range(4):
            got = jnp.dot(
                table_ref[256 * m : 256 * m + 256, :], rows_ref[...], preferred_element_type=F32
            ).astype(BF16)
            out_ref[8 * m : 8 * m + 8, g] = got.reshape(8, 2, 16, NFIT)


def y_transform(core, near, far, table):
    return pl.pallas_call(
        y_kernel,
        out_shape=jax.ShapeDtypeStruct((32, 2, 2, 16, NFIT), BF16),
        in_specs=[pl.BlockSpec(memory_space=pltpu.SMEM)]
        + [pl.BlockSpec(memory_space=pltpu.VMEM)] * 3,
        out_specs=pl.BlockSpec(memory_space=pltpu.VMEM),
        scratch_shapes=[pltpu.VMEM((1024, NFIT), BF16)],
        compiler_params=pltpu.CompilerParams(vmem_limit_bytes=14 << 20),
        name="y_transform",
    )(core, near, far, table)


def gram_kernel(
    core_ref, planes_ref, table_ref, screen_ref, mixed_ref, own_ref, other_ref, coeffs_ref, weighted_ref
):
    mixed = jnp.concatenate([mixed_ref[...]] * 2, axis=1)
    for b in range(2):
        rows = planes_ref[:, b].reshape(1024, NFIT)
        t0, t1, t2, t3 = [
            jnp.dot(table_ref[256 * t : 256 * t + 256, :], rows, preferred_element_type=F32)
            .astype(BF16)
            .astype(F32)
            for t in range(4)
        ]
        outs = (t0 - mixed * t3, mixed * t0 + t3, t2 + mixed * t1, mixed * t2 - t1)
        for o, value in enumerate(outs):
            at = slice(256 * o, 256 * o + 256)
            value = value.astype(BF16)
            coeffs_ref[at, 256 * b : 256 * b + 256] = value
            value = value.astype(F32)
            screen = screen_ref[at, :]
            for h in range(2):
                weighted_ref[h, at, 128 * b : 128 * b + 128] = (
                    value[:, 128 * h : 128 * h + 128] * screen
                ).astype(BF16)
    core = core_ref[0]
    for q in range(2):
        left = coeffs_ref[:, 256 * q : 256 * q + 256]
        for half, out_ref in ((core, own_ref), (1 - core, other_ref)):
            got = kernel_scale * lax.dot_general(
                left, weighted_ref[half], (((0,), (0,)), ((), ())), preferred_element_type=F32
            )
            for b in range(2):
                out_ref[32 * q : 32 * q + 32, b] = got[:, 128 * b : 128 * b + 128].reshape(32, 8, 128)


def gram(core, planes, table, screen, mixed):
    half = jax.ShapeDtypeStruct((N, 2, 8, 128), F32)
    return pl.pallas_call(
        gram_kernel,
        out_shape=(half, half),
        in_specs=[pl.BlockSpec(memory_space=pltpu.SMEM)]
        + [pl.BlockSpec(memory_space=pltpu.VMEM)] * 4,
        out_specs=[pl.BlockSpec(memory_space=pltpu.VMEM)] * 2,
        scratch_shapes=[pltpu.VMEM((1024, 512), BF16), pltpu.VMEM((2, 1024, 256), BF16)],
        compiler_params=pltpu.CompilerParams(vmem_limit_bytes=20 << 20),
        name="gram",
    )(core, planes, table, screen, mixed)


def sibling(block):
    return lax.ppermute(block, "c", [(0, 1), (1, 0)])


def exchange(blocks, axes):
    return lax.all_to_all(blocks, axes, split_axis=0, concat_axis=0, tiled=True)


def on_device(orbitals, points):
    core = lax.axis_index("c")
    batch = lax.axis_index("b")
    chip = lax.axis_index(CHIPS)
    core_word = core.astype(jnp.int32)[None]
    y_pair, z_group = chip // 2, core * 4 + chip % 2 * 2 + batch
    small = pair_table(iota((N, N), 0), iota((N, N), 1)).astype(BF16)
    z_row, z_column = iota((256, 256), 0), iota((256, 256), 1)
    z_half = jnp.where(z_row < 128, core, 1 - core)
    z_table = pair_table(z_half * 32 + z_row % 32, z_column % N)
    z_table = jnp.where(z_row // 32 % 4 == z_column // N, z_table, F32(0.0)).astype(BF16)
    y_big, x_big = expand(small, x_table(y_pair == 0))
    screen, mixed = screen_rows(y_pair, z_group * 4)

    halves = points[0].reshape(2, HALF)
    halves = jnp.where(core == 0, halves, halves[::-1])
    offsets = halves.reshape(1, NFIT) - (chip * 2 + core) * 2048
    orbitals = pltpu.with_memory_space_constraint(orbitals, pltpu.HBM)
    own, other = pick(offsets, orbitals)
    own = exchange((own + sibling(other)).reshape(N, 16, HALF), CHIPS)
    own = jnp.sum(own.astype(F32), axis=0).astype(BF16)
    own = exchange(jnp.broadcast_to(own[None], (N, 16, HALF)), CHIPS).reshape(NORB, HALF)
    own, z_table, y_big, x_big, orbitals = lax.optimization_barrier(
        (own, z_table, y_big, x_big, orbitals)
    )
    held = hold(orbitals)
    near, far = fit(core_word, own, sibling(own), z_table, held)
    planes = y_transform(core_word, near, sibling(far), y_big)
    planes = exchange(planes.reshape(128, 16, NFIT), SAME_CORE).reshape(N, 2, 16, NFIT)
    own, other = gram(core_word, planes, x_big, screen, mixed)
    sums = exchange((own + sibling(other)).reshape(128, 8, 128), SAME_CORE)
    sums = jnp.sum(sums, axis=0).reshape(2, 4, 128)
    mine = lax.dynamic_index_in_dim(sums, core, 0, keepdims=False)
    theirs = sibling(lax.dynamic_index_in_dim(sums, 1 - core, 0, keepdims=False))
    pair = jnp.where(core == 0, jnp.stack([mine, theirs]), jnp.stack([theirs, mine]))
    return pair.transpose(0, 2, 1).reshape(NFIT, 4)


def solution(mesh):
    fine = Mesh(mesh.devices.reshape(2, 4, 8, 2, 2), ("yl", "x", "z", "c", "b"))
    grid = ("yl", "x", "z", "c")
    return jax.shard_map(
        on_device,
        mesh=fine,
        in_specs=(P(None, grid), P("b", None)),
        out_specs=P("b", grid),
        check_vma=False,
    )
```

```python
import math

import jax
import jax.numpy as jnp
from jax import lax
from jax.experimental import pallas as pl
from jax.experimental.pallas import tpu as pltpu
from jax.sharding import Mesh
from jax.sharding import PartitionSpec as P

N = 64
NORB = 1024
NFIT = 256
HALF = NFIT // 2

screen_rate = 0.05
kernel_scale = 16.0

CHIPS = ("yl", "x", "z")
SAME_CORE = ("yl", "x", "z", "b")
F32 = jnp.float32
BF16 = jnp.bfloat16


def signed_freq(values):
    return jnp.where(values < N // 2, values, values - N).astype(F32)


def waves(freq, place):
    angles = (freq * place % N).astype(F32) * F32(2.0 * math.pi / N)
    return jnp.cos(angles) / math.sqrt(N), jnp.sin(angles) / math.sqrt(N)


def iota(shape, dim):
    return lax.broadcasted_iota(jnp.int32, shape, dim)


def pair_table(row, place):
    pair, part = row // 2, row % 2
    freq = jnp.where((pair == 0) & (part == 1), N // 2, pair)
    cosine, sine = waves(freq, place)
    return jnp.where((part == 0) | (pair == 0), cosine, -sine)


def x_table(lone):
    row, column = iota((256, 256), 0), iota((256, 256), 1)
    z_of, e, k = row // 128, row // 64 % 2, row % 64
    z_part, y_part, place = column // 128, column // 64 % 2, column % 64
    k_low = k % 32
    turned = (e == 1) & (k_low == 0)
    freq = jnp.where(lone, jnp.where(turned, N // 2, k_low), k)
    cosine, sine = waves(freq, place)
    both = jnp.where(e == y_part, cosine, jnp.where(e == 0, sine, -sine))
    both = jnp.where(z_of == z_part, both, F32(0.0))
    single = jnp.where((e == 0) | turned, cosine, -sine)
    kept = (y_part == k // 32) & (z_part == jnp.where(turned, 1 - z_of, z_of))
    return jnp.where(lone, jnp.where(kept, single, F32(0.0)), both).astype(BF16)


def screen_rows(y_pair, z_first):
    shape = (1024, 128)
    row = iota(shape, 0)
    out, k, z_pair = row // 256, row // 4 % 64, z_first + row % 4
    lone_y, lone_z = y_pair == 0, z_pair == 0
    k_low = k % 32
    edge = lone_y & (k_low == 0)
    second = (out == 1) | (out == 3)
    kx = jnp.where(lone_y, jnp.where(edge & second, N // 2, k_low), k)
    ky = jnp.where(lone_y, jnp.where(k >= 32, N // 2, 0), y_pair)
    z_late = (out == 2) | jnp.where(edge, out == 3, out == 1)
    kz = jnp.where(lone_z, jnp.where(z_late, N // 2, 0), z_pair)
    fx, fy, fz = signed_freq(kx), signed_freq(ky), signed_freq(kz)
    scaled = screen_rate * (fx * fx + fy * fy + fz * fz)
    positive = scaled > 0
    safe = jnp.where(positive, scaled, F32(1.0))
    screen = jnp.where(positive, -jnp.expm1(-safe) / safe, F32(0.0))
    copies = jnp.where(edge & lone_z, F32(1.0), F32(2.0))
    mixed = jnp.where(lone_z | edge, F32(0.0), F32(1.0))[:256]
    return screen * copies, mixed


def expand_kernel(y_small_ref, x_small_ref, y_ref, x_ref):
    block = pl.program_id(0)
    row = 256 * block + iota((256, 1024), 0)
    column = iota((256, 1024), 1)

    def spread(small, row_of, column_of):
        r = 256 * block + iota((256, small.shape[0]), 0)
        c = iota((small.shape[1], 1024), 1)
        left = jnp.where(row_of(r) == iota(r.shape, 1), F32(1.0), F32(0.0)).astype(BF16)
        right = jnp.where(column_of(c) == iota(c.shape, 0), F32(1.0), F32(0.0)).astype(BF16)
        tall = jnp.dot(left, small, preferred_element_type=F32).astype(BF16)
        return jnp.dot(tall, right, preferred_element_type=F32)

    wide = spread(y_small_ref[...], lambda r: (r >> 5) * 2 + ((r >> 3) & 1), lambda c: c >> 4)
    same = (((row >> 4) & 1) == ((column >> 3) & 1)) & ((row & 7) == (column & 7))
    y_ref[...] = jnp.where(same, wide, F32(0.0)).astype(BF16)
    wide = spread(
        x_small_ref[...],
        lambda r: r >> 2,
        lambda c: (c & 1) * 128 + ((c >> 3) & 1) * 64 + (c >> 4),
    )
    same = (row & 3) == ((column >> 1) & 3)
    x_ref[...] = jnp.where(same, wide, F32(0.0)).astype(BF16)


def expand(y_small, x_small):
    big = jax.ShapeDtypeStruct((1024, 1024), BF16)
    return pl.pallas_call(
        expand_kernel,
        out_shape=(big, big),
        grid=(4,),
        in_specs=[
            pl.BlockSpec((N, N), lambda i: (0, 0)),
            pl.BlockSpec((256, 256), lambda i: (0, 0)),
        ],
        out_specs=[pl.BlockSpec((256, 1024), lambda i: (i, 0))] * 2,
        cost_estimate=pl.CostEstimate(flops=2**31, bytes_accessed=2**22, transcendentals=0),
        compiler_params=pltpu.CompilerParams(vmem_limit_bytes=16 << 20),
        name="expand",
    )(y_small, x_small)


def pick_kernel(place_ref, points_ref, orbitals_ref, own_ref, other_ref, held_ref, hot_ref, got_ref, sem):
    copy = pltpu.make_async_copy(orbitals_ref, held_ref, sem)
    copy.start()
    cell = iota((2048, NFIT), 0) + place_ref[1]
    hot_ref[...] = jnp.where(cell == points_ref[...], F32(1.0), F32(0.0)).astype(BF16)
    copy.wait()
    got_ref[...] = jnp.dot(held_ref[...], hot_ref[...], preferred_element_type=F32).astype(BF16)
    mine = pl.multiple_of(place_ref[0] * HALF, HALF)
    theirs = pl.multiple_of((1 - place_ref[0]) * HALF, HALF)
    own_ref[...] = got_ref[:, pl.ds(mine, HALF)]
    other_ref[...] = got_ref[:, pl.ds(theirs, HALF)]


def pick(place, points, orbitals):
    half = jax.ShapeDtypeStruct((NORB, HALF), BF16)
    vmem = pl.BlockSpec(memory_space=pltpu.VMEM)
    return pl.pallas_call(
        pick_kernel,
        out_shape=(half, half),
        in_specs=[pl.BlockSpec(memory_space=pltpu.SMEM), vmem, pl.BlockSpec(memory_space=pltpu.HBM)],
        out_specs=[vmem] * 2,
        scratch_shapes=[
            pltpu.VMEM((NORB, 2048), BF16),
            pltpu.VMEM((2048, NFIT), BF16),
            pltpu.VMEM((NORB, NFIT), BF16),
            pltpu.SemaphoreType.DMA(()),
        ],
        compiler_params=pltpu.CompilerParams(vmem_limit_bytes=16 << 20),
        name="pick",
    )(place, points, orbitals)


def hold_kernel(orbitals_ref, held_ref, sem):
    copy = pltpu.make_async_copy(orbitals_ref, held_ref, sem)
    copy.start()
    copy.wait()


def hold(orbitals):
    return pl.pallas_call(
        hold_kernel,
        out_shape=jax.ShapeDtypeStruct(orbitals.shape, orbitals.dtype),
        in_specs=[pl.BlockSpec(memory_space=pltpu.HBM)],
        out_specs=pl.BlockSpec(memory_space=pltpu.VMEM),
        scratch_shapes=[pltpu.SemaphoreType.DMA(())],
        compiler_params=pltpu.CompilerParams(vmem_limit_bytes=8 << 20),
        cost_estimate=pl.CostEstimate(flops=0, bytes_accessed=2**23, transcendentals=0),
        name="hold",
    )(orbitals)


def fit_kernel(core_ref, own_ref, other_ref, table_ref, orbitals_ref, near_ref, far_ref, values_ref):
    core = core_ref[0]
    mine = pl.multiple_of(core * HALF, HALF)
    theirs = pl.multiple_of((1 - core) * HALF, HALF)
    values_ref[:, pl.ds(mine, HALF)] = own_ref[...]
    values_ref[:, pl.ds(theirs, HALF)] = other_ref[...]
    density = lax.dot_general(
        orbitals_ref[...], values_ref[...], (((0,), (0,)), ((), ())), preferred_element_type=F32
    )
    fitted = (density * density).astype(BF16)
    for j in range(8):
        half_z = jnp.dot(
            table_ref[...], fitted[256 * j : 256 * j + 256], preferred_element_type=F32
        ).astype(BF16)
        near_ref[4 * j : 4 * j + 4] = half_z[:128].reshape(4, 32, NFIT)
        far_ref[4 * j : 4 * j + 4] = half_z[128:].reshape(4, 32, NFIT)


def fit(core, own, other, table, held):
    half = jax.ShapeDtypeStruct((32, 32, NFIT), BF16)
    vmem = pl.BlockSpec(memory_space=pltpu.VMEM)
    return pl.pallas_call(
        fit_kernel,
        out_shape=(half, half),
        in_specs=[pl.BlockSpec(memory_space=pltpu.SMEM)] + [vmem] * 4,
        out_specs=[vmem] * 2,
        scratch_shapes=[pltpu.VMEM((NORB, NFIT), BF16)],
        compiler_params=pltpu.CompilerParams(vmem_limit_bytes=16 << 20),
        name="fit",
    )(core, own, other, table, held)


def y_kernel(core_ref, near_ref, far_ref, table_ref, out_ref, rows_ref):
    core = core_ref[0]
    mine = pl.multiple_of(core * 512, 512)
    theirs = pl.multiple_of((1 - core) * 512, 512)
    for g in range(2):
        rows_ref[pl.ds(mine, 512), :] = near_ref[:, 16 * g : 16 * g + 16, :].reshape(512, NFIT)
        rows_ref[pl.ds(theirs, 512), :] = far_ref[:, 16 * g : 16 * g + 16, :].reshape(512, NFIT)
        for m in range(4):
            got = jnp.dot(
                table_ref[256 * m : 256 * m + 256, :], rows_ref[...], preferred_element_type=F32
            ).astype(BF16)
            out_ref[8 * m : 8 * m + 8, g] = got.reshape(8, 2, 16, NFIT)


def y_transform(core, near, far, table):
    return pl.pallas_call(
        y_kernel,
        out_shape=jax.ShapeDtypeStruct((32, 2, 2, 16, NFIT), BF16),
        in_specs=[pl.BlockSpec(memory_space=pltpu.SMEM)]
        + [pl.BlockSpec(memory_space=pltpu.VMEM)] * 3,
        out_specs=pl.BlockSpec(memory_space=pltpu.VMEM),
        scratch_shapes=[pltpu.VMEM((1024, NFIT), BF16)],
        compiler_params=pltpu.CompilerParams(vmem_limit_bytes=14 << 20),
        name="y_transform",
    )(core, near, far, table)


def gram_kernel(
    core_ref,
    planes_ref,
    table_ref,
    screens_ref,
    mixed_ref,
    own_ref,
    other_ref,
    coeffs_ref,
    weighted_ref,
    screen_ref,
    sem,
):
    copy = pltpu.make_async_copy(screens_ref, screen_ref, sem)
    copy.start()
    mixed = jnp.concatenate([mixed_ref[...]] * 2, axis=1)
    for b in range(2):
        rows = planes_ref[:, b].reshape(1024, NFIT)
        t0, t1, t2, t3 = [
            jnp.dot(table_ref[256 * t : 256 * t + 256, :], rows, preferred_element_type=F32)
            .astype(BF16)
            .astype(F32)
            for t in range(4)
        ]
        if b == 0:
            copy.wait()
        outs = (t0 - mixed * t3, mixed * t0 + t3, t2 + mixed * t1, mixed * t2 - t1)
        for o, value in enumerate(outs):
            at = slice(256 * o, 256 * o + 256)
            value = value.astype(BF16)
            coeffs_ref[at, 256 * b : 256 * b + 256] = value
            value = value.astype(F32)
            screen = screen_ref[at, :]
            for h in range(2):
                weighted_ref[h, at, 128 * b : 128 * b + 128] = (
                    value[:, 128 * h : 128 * h + 128] * screen
                ).astype(BF16)
    core = core_ref[0]
    for q in range(2):
        left = coeffs_ref[:, 256 * q : 256 * q + 256]
        for half, out_ref in ((core, own_ref), (1 - core, other_ref)):
            got = kernel_scale * lax.dot_general(
                left, weighted_ref[half], (((0,), (0,)), ((), ())), preferred_element_type=F32
            )
            for b in range(2):
                out_ref[32 * q : 32 * q + 32, b] = got[:, 128 * b : 128 * b + 128].reshape(32, 8, 128)


def gram(core, planes, table, screen, mixed):
    half = jax.ShapeDtypeStruct((N, 2, 8, 128), F32)
    return pl.pallas_call(
        gram_kernel,
        out_shape=(half, half),
        in_specs=[pl.BlockSpec(memory_space=pltpu.SMEM)]
        + [pl.BlockSpec(memory_space=pltpu.VMEM)] * 2
        + [pl.BlockSpec(memory_space=pltpu.HBM), pl.BlockSpec(memory_space=pltpu.VMEM)],
        out_specs=[pl.BlockSpec(memory_space=pltpu.VMEM)] * 2,
        scratch_shapes=[
            pltpu.VMEM((1024, 512), BF16),
            pltpu.VMEM((2, 1024, 256), BF16),
            pltpu.VMEM((1024, 128), F32),
            pltpu.SemaphoreType.DMA(()),
        ],
        compiler_params=pltpu.CompilerParams(vmem_limit_bytes=20 << 20),
        name="gram",
    )(core, planes, table, screen, mixed)


def sibling(block):
    return lax.ppermute(block, "c", [(0, 1), (1, 0)])


def exchange(blocks, axes):
    return lax.all_to_all(blocks, axes, split_axis=0, concat_axis=0, tiled=True)


def on_device(orbitals, points):
    core = lax.axis_index("c")
    batch = lax.axis_index("b")
    chip = lax.axis_index(CHIPS)
    core_word = core.astype(jnp.int32)[None]
    y_pair, z_group = chip // 2, core * 4 + chip % 2 * 2 + batch
    small = pair_table(iota((N, N), 0), iota((N, N), 1)).astype(BF16)
    z_row, z_column = iota((256, 256), 0), iota((256, 256), 1)
    z_half = jnp.where(z_row < 128, core, 1 - core)
    z_table = pair_table(z_half * 32 + z_row % 32, z_column % N)
    z_table = jnp.where(z_row // 32 % 4 == z_column // N, z_table, F32(0.0)).astype(BF16)
    y_big, x_big = expand(small, x_table(y_pair == 0))
    screen, mixed = screen_rows(y_pair, z_group * 4)
    screen = pltpu.with_memory_space_constraint(screen, pltpu.HBM)

    place = jnp.stack([core, (chip * 2 + core) * 2048]).astype(jnp.int32)
    orbitals = pltpu.with_memory_space_constraint(orbitals, pltpu.HBM)
    own, other = pick(place, points, orbitals)
    own = exchange((own + sibling(other)).reshape(N, 16, HALF), CHIPS)
    own = jnp.sum(own.astype(F32), axis=0).astype(BF16)
    own = exchange(jnp.broadcast_to(own[None], (N, 16, HALF)), CHIPS).reshape(NORB, HALF)
    own, z_table, y_big, x_big, orbitals = lax.optimization_barrier(
        (own, z_table, y_big, x_big, orbitals)
    )
    held = hold(orbitals)
    near, far = fit(core_word, own, sibling(own), z_table, held)
    planes = y_transform(core_word, near, sibling(far), y_big)
    planes = exchange(planes.reshape(128, 16, NFIT), SAME_CORE).reshape(N, 2, 16, NFIT)
    own, other = gram(core_word, planes, x_big, screen, mixed)
    sums = exchange((own + sibling(other)).reshape(128, 8, 128), SAME_CORE)
    sums = jnp.sum(sums, axis=0).reshape(2, 4, 128)
    mine = lax.dynamic_index_in_dim(sums, core, 0, keepdims=False)
    theirs = sibling(lax.dynamic_index_in_dim(sums, 1 - core, 0, keepdims=False))
    pair = jnp.where(core == 0, jnp.stack([mine, theirs]), jnp.stack([theirs, mine]))
    return pair.transpose(0, 2, 1).reshape(NFIT, 4)


def solution(mesh):
    fine = Mesh(mesh.devices.reshape(2, 4, 8, 2, 2), ("yl", "x", "z", "c", "b"))
    grid = ("yl", "x", "z", "c")
    return jax.shard_map(
        on_device,
        mesh=fine,
        in_specs=(P(None, grid), P("b", None)),
        out_specs=P("b", grid),
        check_vma=False,
    )
```

```python
import math

import jax
import jax.numpy as jnp
from jax import lax
from jax.experimental import pallas as pl
from jax.experimental.pallas import tpu as pltpu
from jax.sharding import Mesh
from jax.sharding import PartitionSpec as P

N = 64
NORB = 1024
NFIT = 256
HALF = NORB // 2
CHIP_SLOTS = 16
LINE_SLOTS = 64

screen_rate = 0.05
kernel_scale = 16.0

CHIPS = ("yl", "x", "z")
LINES = ("yl", "x")
SAME_CORE = ("yl", "x", "z", "b")
F32 = jnp.float32
BF16 = jnp.bfloat16


def signed_freq(values):
    return jnp.where(values < N // 2, values, values - N).astype(F32)


def waves(freq, place):
    angles = (freq * place % N).astype(F32) * F32(2.0 * math.pi / N)
    return jnp.cos(angles) / math.sqrt(N), jnp.sin(angles) / math.sqrt(N)


def iota(shape, dim):
    return lax.broadcasted_iota(jnp.int32, shape, dim)


def pair_table(row, place):
    pair, part = row // 2, row % 2
    freq = jnp.where((pair == 0) & (part == 1), N // 2, pair)
    cosine, sine = waves(freq, place)
    return jnp.where((part == 0) | (pair == 0), cosine, -sine)


def x_table(lone):
    row, column = iota((256, 256), 0), iota((256, 256), 1)
    z_of, e, k = row // 128, row // 64 % 2, row % 64
    z_part, y_part, place = column // 128, column // 64 % 2, column % 64
    k_low = k % 32
    turned = (e == 1) & (k_low == 0)
    freq = jnp.where(lone, jnp.where(turned, N // 2, k_low), k)
    cosine, sine = waves(freq, place)
    both = jnp.where(e == y_part, cosine, jnp.where(e == 0, sine, -sine))
    both = jnp.where(z_of == z_part, both, F32(0.0))
    single = jnp.where((e == 0) | turned, cosine, -sine)
    kept = (y_part == k // 32) & (z_part == jnp.where(turned, 1 - z_of, z_of))
    return jnp.where(lone, jnp.where(kept, single, F32(0.0)), both).astype(BF16)


def screen_rows(y_pair, z_first):
    shape = (1024, 128)
    row = iota(shape, 0)
    out, k, z_pair = row // 256, row // 4 % 64, z_first + row % 4
    lone_y, lone_z = y_pair == 0, z_pair == 0
    k_low = k % 32
    edge = lone_y & (k_low == 0)
    second = (out == 1) | (out == 3)
    kx = jnp.where(lone_y, jnp.where(edge & second, N // 2, k_low), k)
    ky = jnp.where(lone_y, jnp.where(k >= 32, N // 2, 0), y_pair)
    z_late = (out == 2) | jnp.where(edge, out == 3, out == 1)
    kz = jnp.where(lone_z, jnp.where(z_late, N // 2, 0), z_pair)
    fx, fy, fz = signed_freq(kx), signed_freq(ky), signed_freq(kz)
    scaled = screen_rate * (fx * fx + fy * fy + fz * fz)
    positive = scaled > 0
    safe = jnp.where(positive, scaled, F32(1.0))
    screen = jnp.where(positive, -jnp.expm1(-safe) / safe, F32(0.0))
    copies = jnp.where(edge & lone_z, F32(1.0), F32(2.0))
    mixed = jnp.where(lone_z | edge, F32(0.0), F32(1.0))[:256]
    return screen * copies, mixed


def spread(small, row_of, column_of, first, rows, columns):
    r = first + iota((rows, small.shape[0]), 0)
    c = iota((small.shape[1], columns), 1)
    left = jnp.where(row_of(r) == iota(r.shape, 1), F32(1.0), F32(0.0)).astype(BF16)
    right = jnp.where(column_of(c) == iota(c.shape, 0), F32(1.0), F32(0.0)).astype(BF16)
    tall = jnp.dot(left, small, preferred_element_type=F32).astype(BF16)
    return jnp.dot(tall, right, preferred_element_type=F32)


def expand_yz_kernel(core_ref, small_ref, z_ref, y_ref):
    core = core_ref[0]
    small = small_ref[...]
    row, column = iota((256, 256), 0), iota((256, 256), 1)
    wide = spread(
        small,
        lambda r: jnp.where(r < 128, core, 1 - core) * 32 + (r & 31),
        lambda c: c & 63,
        0,
        256,
        256,
    )
    same = ((row >> 5) & 3) == (column >> 6)
    z_ref[...] = jnp.where(same, wide, F32(0.0)).astype(BF16)
    column = iota((256, 1024), 1)
    for block in range(4):
        row = 256 * block + iota((256, 1024), 0)
        wide = spread(
            small, lambda r: (r >> 5) * 2 + ((r >> 3) & 1), lambda c: c >> 4, 256 * block, 256, 1024
        )
        same = (((row >> 4) & 1) == ((column >> 3) & 1)) & ((row & 7) == (column & 7))
        y_ref[256 * block : 256 * block + 256, :] = jnp.where(same, wide, F32(0.0)).astype(BF16)


def expand_yz(core, small):
    vmem = pl.BlockSpec(memory_space=pltpu.VMEM)
    return pl.pallas_call(
        expand_yz_kernel,
        out_shape=(
            jax.ShapeDtypeStruct((256, 256), BF16),
            jax.ShapeDtypeStruct((1024, 1024), BF16),
        ),
        in_specs=[pl.BlockSpec(memory_space=pltpu.SMEM), vmem],
        out_specs=[vmem] * 2,
        compiler_params=pltpu.CompilerParams(vmem_limit_bytes=16 << 20),
        cost_estimate=pl.CostEstimate(flops=2**30, bytes_accessed=2**21, transcendentals=0),
        name="expand_yz",
    )(core, small)


def expand_x_kernel(small_ref, x_ref):
    column = iota((256, 1024), 1)
    for block in range(4):
        row = 256 * block + iota((256, 1024), 0)
        wide = spread(
            small_ref[...],
            lambda r: r >> 2,
            lambda c: (c & 1) * 128 + ((c >> 3) & 1) * 64 + (c >> 4),
            256 * block,
            256,
            1024,
        )
        same = (row & 3) == ((column >> 1) & 3)
        x_ref[256 * block : 256 * block + 256, :] = jnp.where(same, wide, F32(0.0)).astype(BF16)


def expand_x(small):
    vmem = pl.BlockSpec(memory_space=pltpu.VMEM)
    return pl.pallas_call(
        expand_x_kernel,
        out_shape=jax.ShapeDtypeStruct((1024, 1024), BF16),
        in_specs=[vmem],
        out_specs=vmem,
        compiler_params=pltpu.CompilerParams(vmem_limit_bytes=16 << 20),
        cost_estimate=pl.CostEstimate(flops=2**31, bytes_accessed=2**21, transcendentals=0),
        name="expand_x",
    )(small)


def pick_kernel(
    place_ref, points_ref, orbitals_ref, own_ref, other_ref, ranks_ref, merge_ref, held_ref, got_ref, sem
):
    copy = pltpu.make_async_copy(orbitals_ref, held_ref, sem)
    copy.start()
    core, chip, base = place_ref[0], place_ref[1], place_ref[2]
    points = points_ref[...]
    columns = jnp.broadcast_to(points.astype(F32), (128, NFIT)).T.astype(jnp.int32)
    column = jnp.concatenate([columns] * 2, axis=1)
    before_row = iota((NFIT, NFIT), 0) < iota((NFIT, NFIT), 1)
    before_column = iota((NFIT, NFIT), 1) < iota((NFIT, NFIT), 0)

    def count(matches, axis):
        return jnp.sum(jnp.where(matches, F32(1.0), F32(0.0)), axis=axis, keepdims=True)

    same_chip = (column >> 12) == (points >> 12)
    same_line = (column >> 15) == (points >> 15)
    chip_rank = count(same_chip & before_row, 0).astype(jnp.int32)
    line_rank = count(same_line & before_row, 0).astype(jnp.int32)
    rank_column = count(same_chip & before_column, 1).astype(jnp.int32)
    ranks_ref[0:1, :] = chip_rank
    ranks_ref[1:2, :] = line_rank
    ranks_ref[2:3, :] = points >> 15

    slot = iota((NFIT, 128), 1)
    chosen = ((columns >> 12) == chip) & (rank_column == slot)
    offsets = jnp.max(
        jnp.where(chosen, (columns - base).astype(F32), F32(-1.0)), axis=0, keepdims=True
    ).astype(jnp.int32)
    hot = jnp.where(iota((2048, 128), 0) == offsets, F32(1.0), F32(0.0)).astype(BF16)

    to_slot = ((points >> 15) == (chip >> 3)) & (line_rank == iota((LINE_SLOTS, NFIT), 0))
    from_slot = (((columns >> 12) & 7) == (slot >> 4)) & (rank_column == (slot & 15))
    merge_ref[...] = jnp.dot(
        jnp.where(to_slot, F32(1.0), F32(0.0)).astype(BF16),
        jnp.where(from_slot, F32(1.0), F32(0.0)).astype(BF16),
        preferred_element_type=F32,
    ).astype(BF16)

    copy.wait()
    got = jnp.dot(held_ref[...], hot, preferred_element_type=F32)
    got_ref[...] = got.T[:CHIP_SLOTS].astype(BF16)
    own_ref[...] = got_ref[:, pl.ds(pl.multiple_of(core * HALF, HALF), HALF)]
    other_ref[...] = got_ref[:, pl.ds(pl.multiple_of((1 - core) * HALF, HALF), HALF)]


def pick(place, points, orbitals):
    half = jax.ShapeDtypeStruct((CHIP_SLOTS, HALF), BF16)
    vmem = pl.BlockSpec(memory_space=pltpu.VMEM)
    return pl.pallas_call(
        pick_kernel,
        out_shape=(
            half,
            half,
            jax.ShapeDtypeStruct((8, NFIT), jnp.int32),
            jax.ShapeDtypeStruct((LINE_SLOTS, 128), BF16),
        ),
        in_specs=[pl.BlockSpec(memory_space=pltpu.SMEM), vmem, pl.BlockSpec(memory_space=pltpu.HBM)],
        out_specs=[vmem] * 4,
        scratch_shapes=[
            pltpu.VMEM((NORB, 2048), BF16),
            pltpu.VMEM((CHIP_SLOTS, NORB), BF16),
            pltpu.SemaphoreType.DMA(()),
        ],
        compiler_params=pltpu.CompilerParams(vmem_limit_bytes=16 << 20),
        name="pick",
    )(place, points, orbitals)


def merge_kernel(merge_ref, slots_ref, out_ref):
    got = jnp.dot(
        merge_ref[...], slots_ref[...].reshape(128, HALF), preferred_element_type=F32
    ).astype(BF16)
    for i in range(8):
        out_ref[i] = got


def merge(table, slots):
    vmem = pl.BlockSpec(memory_space=pltpu.VMEM)
    return pl.pallas_call(
        merge_kernel,
        out_shape=jax.ShapeDtypeStruct((8, LINE_SLOTS, HALF), BF16),
        in_specs=[vmem] * 2,
        out_specs=vmem,
        compiler_params=pltpu.CompilerParams(vmem_limit_bytes=8 << 20),
        name="merge",
    )(table, slots)


def order_kernel(ranks_ref, slots_ref, out_ref):
    row = iota((8 * LINE_SLOTS, NFIT), 0)
    here = ((row >> 6) == ranks_ref[2:3, :]) & ((row & 63) == ranks_ref[1:2, :])
    out_ref[...] = lax.dot_general(
        slots_ref[...].reshape(8 * LINE_SLOTS, HALF),
        jnp.where(here, F32(1.0), F32(0.0)).astype(BF16),
        (((0,), (0,)), ((), ())),
        preferred_element_type=F32,
    ).astype(BF16)


def order(ranks, slots):
    vmem = pl.BlockSpec(memory_space=pltpu.VMEM)
    return pl.pallas_call(
        order_kernel,
        out_shape=jax.ShapeDtypeStruct((HALF, NFIT), BF16),
        in_specs=[vmem] * 2,
        out_specs=vmem,
        compiler_params=pltpu.CompilerParams(vmem_limit_bytes=8 << 20),
        name="order",
    )(ranks, slots)


def any_points(points, orbitals, core, base):
    cell = iota((2048, NFIT), 0) + base
    hot = jnp.where(cell == points, F32(1.0), F32(0.0)).astype(BF16)
    got = jnp.dot(orbitals, hot, preferred_element_type=F32).astype(BF16)
    own = lax.dynamic_slice_in_dim(got, core * HALF, HALF, 0)
    other = lax.dynamic_slice_in_dim(got, (1 - core) * HALF, HALF, 0)
    own = exchange((own + sibling(other)).reshape(N, 8, NFIT), CHIPS)
    own = jnp.sum(own.astype(F32), axis=0).astype(BF16)
    return exchange(jnp.broadcast_to(own[None], (N, 8, NFIT)), CHIPS).reshape(HALF, NFIT)


def hold_kernel(orbitals_ref, held_ref, sem):
    copy = pltpu.make_async_copy(orbitals_ref, held_ref, sem)
    copy.start()
    copy.wait()


def hold(orbitals):
    return pl.pallas_call(
        hold_kernel,
        out_shape=jax.ShapeDtypeStruct(orbitals.shape, orbitals.dtype),
        in_specs=[pl.BlockSpec(memory_space=pltpu.HBM)],
        out_specs=pl.BlockSpec(memory_space=pltpu.VMEM),
        scratch_shapes=[pltpu.SemaphoreType.DMA(())],
        compiler_params=pltpu.CompilerParams(vmem_limit_bytes=8 << 20),
        cost_estimate=pl.CostEstimate(flops=0, bytes_accessed=2**23, transcendentals=0),
        name="hold",
    )(orbitals)


def fit_kernel(core_ref, own_ref, other_ref, table_ref, orbitals_ref, near_ref, far_ref, values_ref):
    core = core_ref[0]
    mine = pl.multiple_of(core * HALF, HALF)
    theirs = pl.multiple_of((1 - core) * HALF, HALF)
    values_ref[pl.ds(mine, HALF), :] = own_ref[...]
    values_ref[pl.ds(theirs, HALF), :] = other_ref[...]
    density = lax.dot_general(
        orbitals_ref[...], values_ref[...], (((0,), (0,)), ((), ())), preferred_element_type=F32
    )
    fitted = (density * density).astype(BF16)
    for j in range(8):
        half_z = jnp.dot(
            table_ref[...], fitted[256 * j : 256 * j + 256], preferred_element_type=F32
        ).astype(BF16)
        near_ref[4 * j : 4 * j + 4] = half_z[:128].reshape(4, 32, NFIT)
        far_ref[4 * j : 4 * j + 4] = half_z[128:].reshape(4, 32, NFIT)


def fit(core, own, other, table, held):
    half = jax.ShapeDtypeStruct((32, 32, NFIT), BF16)
    vmem = pl.BlockSpec(memory_space=pltpu.VMEM)
    return pl.pallas_call(
        fit_kernel,
        out_shape=(half, half),
        in_specs=[pl.BlockSpec(memory_space=pltpu.SMEM)] + [vmem] * 4,
        out_specs=[vmem] * 2,
        scratch_shapes=[pltpu.VMEM((NORB, NFIT), BF16)],
        compiler_params=pltpu.CompilerParams(vmem_limit_bytes=16 << 20),
        name="fit",
    )(core, own, other, table, held)


def y_kernel(core_ref, near_ref, far_ref, table_ref, out_ref, rows_ref):
    core = core_ref[0]
    mine = pl.multiple_of(core * 512, 512)
    theirs = pl.multiple_of((1 - core) * 512, 512)
    for g in range(2):
        rows_ref[pl.ds(mine, 512), :] = near_ref[:, 16 * g : 16 * g + 16, :].reshape(512, NFIT)
        rows_ref[pl.ds(theirs, 512), :] = far_ref[:, 16 * g : 16 * g + 16, :].reshape(512, NFIT)
        for m in range(4):
            got = jnp.dot(
                table_ref[256 * m : 256 * m + 256, :], rows_ref[...], preferred_element_type=F32
            ).astype(BF16)
            out_ref[8 * m : 8 * m + 8, g] = got.reshape(8, 2, 16, NFIT)


def y_transform(core, near, far, table):
    return pl.pallas_call(
        y_kernel,
        out_shape=jax.ShapeDtypeStruct((32, 2, 2, 16, NFIT), BF16),
        in_specs=[pl.BlockSpec(memory_space=pltpu.SMEM)]
        + [pl.BlockSpec(memory_space=pltpu.VMEM)] * 3,
        out_specs=pl.BlockSpec(memory_space=pltpu.VMEM),
        scratch_shapes=[pltpu.VMEM((1024, NFIT), BF16)],
        compiler_params=pltpu.CompilerParams(vmem_limit_bytes=14 << 20),
        name="y_transform",
    )(core, near, far, table)


def gram_kernel(
    core_ref,
    planes_ref,
    table_ref,
    screens_ref,
    mixed_ref,
    own_ref,
    other_ref,
    coeffs_ref,
    weighted_ref,
    screen_ref,
    sem,
):
    copy = pltpu.make_async_copy(screens_ref, screen_ref, sem)
    copy.start()
    mixed = jnp.concatenate([mixed_ref[...]] * 2, axis=1)
    for b in range(2):
        rows = planes_ref[:, b].reshape(1024, NFIT)
        t0, t1, t2, t3 = [
            jnp.dot(table_ref[256 * t : 256 * t + 256, :], rows, preferred_element_type=F32)
            .astype(BF16)
            .astype(F32)
            for t in range(4)
        ]
        if b == 0:
            copy.wait()
        outs = (t0 - mixed * t3, mixed * t0 + t3, t2 + mixed * t1, mixed * t2 - t1)
        for o, value in enumerate(outs):
            at = slice(256 * o, 256 * o + 256)
            value = value.astype(BF16)
            coeffs_ref[at, 256 * b : 256 * b + 256] = value
            value = value.astype(F32)
            screen = screen_ref[at, :]
            for h in range(2):
                weighted_ref[h, at, 128 * b : 128 * b + 128] = (
                    value[:, 128 * h : 128 * h + 128] * screen
                ).astype(BF16)
    core = core_ref[0]
    for q in range(2):
        left = coeffs_ref[:, 256 * q : 256 * q + 256]
        for half, out_ref in ((core, own_ref), (1 - core, other_ref)):
            got = kernel_scale * lax.dot_general(
                left, weighted_ref[half], (((0,), (0,)), ((), ())), preferred_element_type=F32
            )
            for b in range(2):
                out_ref[32 * q : 32 * q + 32, b] = got[:, 128 * b : 128 * b + 128].reshape(32, 8, 128)


def gram(core, planes, table, screen, mixed):
    half = jax.ShapeDtypeStruct((N, 2, 8, 128), F32)
    return pl.pallas_call(
        gram_kernel,
        out_shape=(half, half),
        in_specs=[pl.BlockSpec(memory_space=pltpu.SMEM)]
        + [pl.BlockSpec(memory_space=pltpu.VMEM)] * 2
        + [pl.BlockSpec(memory_space=pltpu.HBM), pl.BlockSpec(memory_space=pltpu.VMEM)],
        out_specs=[pl.BlockSpec(memory_space=pltpu.VMEM)] * 2,
        scratch_shapes=[
            pltpu.VMEM((1024, 512), BF16),
            pltpu.VMEM((2, 1024, 256), BF16),
            pltpu.VMEM((1024, 128), F32),
            pltpu.SemaphoreType.DMA(()),
        ],
        compiler_params=pltpu.CompilerParams(vmem_limit_bytes=20 << 20),
        name="gram",
    )(core, planes, table, screen, mixed)


def sibling(block):
    return lax.ppermute(block, "c", [(0, 1), (1, 0)])


def exchange(blocks, axes):
    return lax.all_to_all(blocks, axes, split_axis=0, concat_axis=0, tiled=True)


def on_device(orbitals, points):
    core = lax.axis_index("c")
    batch = lax.axis_index("b")
    chip = lax.axis_index(CHIPS)
    core_word = core.astype(jnp.int32)[None]
    y_pair, z_group = chip // 2, core * 4 + chip % 2 * 2 + batch
    base = (chip * 2 + core) * 2048
    place = jnp.stack([core, chip, base]).astype(jnp.int32)
    own, other, ranks, merge_table = pick(place, points, orbitals)
    own = own + sibling(other)
    slots = exchange(jnp.broadcast_to(own[None], (8, CHIP_SLOTS, HALF)), ("z",))

    small = pair_table(iota((N, N), 0), iota((N, N), 1)).astype(BF16)
    z_table, y_big = expand_yz(core_word, small)
    full = (jnp.max(ranks[0]) >= CHIP_SLOTS) | (jnp.max(ranks[1]) >= LINE_SLOTS)
    full = jnp.where(full, F32(1.0), F32(0.0))[None]
    slots, z_table, y_big, full = lax.optimization_barrier((slots, z_table, y_big, full))
    slots = exchange(merge(merge_table, slots), LINES)
    full = full + lax.ppermute(full, "b", [(0, 1), (1, 0)])
    x_small = x_table(y_pair == 0)
    slots, full, x_small, orbitals = lax.optimization_barrier((slots, full, x_small, orbitals))
    own = order(ranks, slots)
    own = lax.cond(
        full[0] > 0,
        lambda o: any_points(points, orbitals, core, base),
        lambda o: o,
        own,
    )
    held = hold(orbitals)
    near, far = fit(core_word, own, sibling(own), z_table, held)
    x_big = expand_x(x_small)
    screen, mixed = screen_rows(y_pair, z_group * 4)
    screen = pltpu.with_memory_space_constraint(screen, pltpu.HBM)
    planes = y_transform(core_word, near, sibling(far), y_big)
    planes = exchange(planes.reshape(128, 16, NFIT), SAME_CORE).reshape(N, 2, 16, NFIT)
    own, other = gram(core_word, planes, x_big, screen, mixed)
    sums = exchange((own + sibling(other)).reshape(128, 8, 128), SAME_CORE)
    sums = jnp.sum(sums, axis=0).reshape(2, 4, 128)
    mine = lax.dynamic_index_in_dim(sums, core, 0, keepdims=False)
    theirs = sibling(lax.dynamic_index_in_dim(sums, 1 - core, 0, keepdims=False))
    pair = jnp.where(core == 0, jnp.stack([mine, theirs]), jnp.stack([theirs, mine]))
    return pair.transpose(0, 2, 1).reshape(NFIT, 4)


def solution(mesh):
    fine = Mesh(mesh.devices.reshape(2, 4, 8, 2, 2), ("yl", "x", "z", "c", "b"))
    grid = ("yl", "x", "z", "c")
    return jax.shard_map(
        on_device,
        mesh=fine,
        in_specs=(P(None, grid), P("b", None)),
        out_specs=P("b", grid),
        check_vma=False,
    )
```

```python
import math

import jax
import jax.numpy as jnp
from jax import lax
from jax.experimental import pallas as pl
from jax.experimental.pallas import tpu as pltpu
from jax.sharding import Mesh
from jax.sharding import PartitionSpec as P

N = 64
NORB = 1024
NFIT = 256
HALF = NORB // 2
CHIP_SLOTS = 16
LINE_SLOTS = 64

screen_rate = 0.05
kernel_scale = 16.0

CHIPS = ("yl", "x", "z")
LINES = ("yl", "x")
SAME_CORE = ("b", "x", "z", "yl")
F32 = jnp.float32
BF16 = jnp.bfloat16


def signed_freq(values):
    return jnp.where(values < N // 2, values, values - N).astype(F32)


def waves(freq, place):
    angles = (freq * place % N).astype(F32) * F32(2.0 * math.pi / N)
    return jnp.cos(angles) / math.sqrt(N), jnp.sin(angles) / math.sqrt(N)


def iota(shape, dim):
    return lax.broadcasted_iota(jnp.int32, shape, dim)


def pair_table(row, place):
    pair, part = row // 2, row % 2
    freq = jnp.where((pair == 0) & (part == 1), N // 2, pair)
    cosine, sine = waves(freq, place)
    return jnp.where((part == 0) | (pair == 0), cosine, -sine)


def x_table(lone):
    row, column = iota((256, 256), 0), iota((256, 256), 1)
    z_of, e, k = row // 128, row // 64 % 2, row % 64
    z_part, y_part, chip = column // 128, column // 64 % 2, column % 64
    place = chip % 2 * 32 + chip // 16 * 8 + chip // 2 % 8
    k_low = k % 32
    turned = (e == 1) & (k_low == 0)
    freq = jnp.where(lone, jnp.where(turned, N // 2, k_low), k)
    cosine, sine = waves(freq, place)
    both = jnp.where(e == y_part, cosine, jnp.where(e == 0, sine, -sine))
    both = jnp.where(z_of == z_part, both, F32(0.0))
    single = jnp.where((e == 0) | turned, cosine, -sine)
    kept = (y_part == k // 32) & (z_part == jnp.where(turned, 1 - z_of, z_of))
    return jnp.where(lone, jnp.where(kept, single, F32(0.0)), both).astype(BF16)


def screen_rows(y_pair, z_first):
    shape = (1024, 128)
    row = iota(shape, 0)
    out, k, z_pair = row // 256, row // 4 % 64, z_first + row % 4
    lone_y, lone_z = y_pair == 0, z_pair == 0
    k_low = k % 32
    edge = lone_y & (k_low == 0)
    second = (out == 1) | (out == 3)
    kx = jnp.where(lone_y, jnp.where(edge & second, N // 2, k_low), k)
    ky = jnp.where(lone_y, jnp.where(k >= 32, N // 2, 0), y_pair)
    z_late = (out == 2) | jnp.where(edge, out == 3, out == 1)
    kz = jnp.where(lone_z, jnp.where(z_late, N // 2, 0), z_pair)
    fx, fy, fz = signed_freq(kx), signed_freq(ky), signed_freq(kz)
    scaled = screen_rate * (fx * fx + fy * fy + fz * fz)
    positive = scaled > 0
    safe = jnp.where(positive, scaled, F32(1.0))
    screen = jnp.where(positive, -jnp.expm1(-safe) / safe, F32(0.0))
    copies = jnp.where(edge & lone_z, F32(1.0), F32(2.0))
    mixed = jnp.where(lone_z | edge, F32(0.0), F32(1.0))[:256]
    return screen * copies, mixed


def spread(small, row_of, column_of, first, rows, columns):
    r = first + iota((rows, small.shape[0]), 0)
    c = iota((small.shape[1], columns), 1)
    left = jnp.where(row_of(r) == iota(r.shape, 1), F32(1.0), F32(0.0)).astype(BF16)
    right = jnp.where(column_of(c) == iota(c.shape, 0), F32(1.0), F32(0.0)).astype(BF16)
    tall = jnp.dot(left, small, preferred_element_type=F32).astype(BF16)
    return jnp.dot(tall, right, preferred_element_type=F32)


def expand_yz_kernel(core_ref, small_ref, z_ref, y_ref):
    core = core_ref[0]
    small = small_ref[...]
    row, column = iota((256, 256), 0), iota((256, 256), 1)
    wide = spread(
        small,
        lambda r: jnp.where(r < 128, core, 1 - core) * 32 + (r & 31),
        lambda c: c & 63,
        0,
        256,
        256,
    )
    same = ((row >> 5) & 3) == (column >> 6)
    z_ref[...] = jnp.where(same, wide, F32(0.0)).astype(BF16)
    column = iota((256, 1024), 1)
    for block in range(4):
        row = 256 * block + iota((256, 1024), 0)
        wide = spread(
            small, lambda r: (r >> 5) * 2 + ((r >> 3) & 1), lambda c: c >> 4, 256 * block, 256, 1024
        )
        same = (((row >> 4) & 1) == ((column >> 3) & 1)) & ((row & 7) == (column & 7))
        y_ref[256 * block : 256 * block + 256, :] = jnp.where(same, wide, F32(0.0)).astype(BF16)


def expand_yz(core, small):
    vmem = pl.BlockSpec(memory_space=pltpu.VMEM)
    return pl.pallas_call(
        expand_yz_kernel,
        out_shape=(
            jax.ShapeDtypeStruct((256, 256), BF16),
            jax.ShapeDtypeStruct((1024, 1024), BF16),
        ),
        in_specs=[pl.BlockSpec(memory_space=pltpu.SMEM), vmem],
        out_specs=[vmem] * 2,
        compiler_params=pltpu.CompilerParams(vmem_limit_bytes=16 << 20),
        cost_estimate=pl.CostEstimate(flops=2**30, bytes_accessed=2**21, transcendentals=0),
        name="expand_yz",
    )(core, small)


def expand_x_kernel(small_ref, x_ref):
    column = iota((256, 1024), 1)
    for block in range(4):
        row = 256 * block + iota((256, 1024), 0)
        wide = spread(
            small_ref[...],
            lambda r: r >> 2,
            lambda c: (c & 1) * 128 + ((c >> 3) & 1) * 64 + (c >> 4),
            256 * block,
            256,
            1024,
        )
        same = (row & 3) == ((column >> 1) & 3)
        x_ref[256 * block : 256 * block + 256, :] = jnp.where(same, wide, F32(0.0)).astype(BF16)


def expand_x(small):
    vmem = pl.BlockSpec(memory_space=pltpu.VMEM)
    return pl.pallas_call(
        expand_x_kernel,
        out_shape=jax.ShapeDtypeStruct((1024, 1024), BF16),
        in_specs=[vmem],
        out_specs=vmem,
        compiler_params=pltpu.CompilerParams(vmem_limit_bytes=16 << 20),
        cost_estimate=pl.CostEstimate(flops=2**31, bytes_accessed=2**21, transcendentals=0),
        name="expand_x",
    )(small)


def pick_kernel(
    place_ref, points_ref, orbitals_ref, own_ref, other_ref, ranks_ref, merge_ref, held_ref, got_ref, sem
):
    copy = pltpu.make_async_copy(orbitals_ref, held_ref, sem)
    copy.start()
    core, chip, base = place_ref[0], place_ref[1], place_ref[2]
    points = points_ref[...]
    columns = jnp.broadcast_to(points.astype(F32), (128, NFIT)).T.astype(jnp.int32)
    column = jnp.concatenate([columns] * 2, axis=1)
    before_row = iota((NFIT, NFIT), 0) < iota((NFIT, NFIT), 1)
    before_column = iota((NFIT, NFIT), 1) < iota((NFIT, NFIT), 0)

    def count(matches, axis):
        return jnp.sum(jnp.where(matches, F32(1.0), F32(0.0)), axis=axis, keepdims=True)

    same_chip = (column >> 12) == (points >> 12)
    same_line = (column >> 15) == (points >> 15)
    chip_rank = count(same_chip & before_row, 0).astype(jnp.int32)
    line_rank = count(same_line & before_row, 0).astype(jnp.int32)
    rank_column = count(same_chip & before_column, 1).astype(jnp.int32)
    ranks_ref[0:1, :] = chip_rank
    ranks_ref[1:2, :] = line_rank
    ranks_ref[2:3, :] = points >> 15

    slot = iota((NFIT, 128), 1)
    chosen = ((columns >> 12) == chip) & (rank_column == slot)
    offsets = jnp.max(
        jnp.where(chosen, (columns - base).astype(F32), F32(-1.0)), axis=0, keepdims=True
    ).astype(jnp.int32)
    hot = jnp.where(iota((2048, 128), 0) == offsets, F32(1.0), F32(0.0)).astype(BF16)

    to_slot = ((points >> 15) == (chip >> 3)) & (line_rank == iota((LINE_SLOTS, NFIT), 0))
    from_slot = (((columns >> 12) & 7) == (slot >> 4)) & (rank_column == (slot & 15))
    merge_ref[...] = jnp.dot(
        jnp.where(to_slot, F32(1.0), F32(0.0)).astype(BF16),
        jnp.where(from_slot, F32(1.0), F32(0.0)).astype(BF16),
        preferred_element_type=F32,
    ).astype(BF16)

    copy.wait()
    got = jnp.dot(held_ref[...], hot, preferred_element_type=F32)
    got_ref[...] = got.T[:CHIP_SLOTS].astype(BF16)
    own_ref[...] = got_ref[:, pl.ds(pl.multiple_of(core * HALF, HALF), HALF)]
    other_ref[...] = got_ref[:, pl.ds(pl.multiple_of((1 - core) * HALF, HALF), HALF)]


def pick(place, points, orbitals):
    half = jax.ShapeDtypeStruct((CHIP_SLOTS, HALF), BF16)
    vmem = pl.BlockSpec(memory_space=pltpu.VMEM)
    return pl.pallas_call(
        pick_kernel,
        out_shape=(
            half,
            half,
            jax.ShapeDtypeStruct((8, NFIT), jnp.int32),
            jax.ShapeDtypeStruct((LINE_SLOTS, 128), BF16),
        ),
        in_specs=[pl.BlockSpec(memory_space=pltpu.SMEM), vmem, pl.BlockSpec(memory_space=pltpu.HBM)],
        out_specs=[vmem] * 4,
        scratch_shapes=[
            pltpu.VMEM((NORB, 2048), BF16),
            pltpu.VMEM((CHIP_SLOTS, NORB), BF16),
            pltpu.SemaphoreType.DMA(()),
        ],
        compiler_params=pltpu.CompilerParams(vmem_limit_bytes=16 << 20),
        name="pick",
    )(place, points, orbitals)


def merge_kernel(merge_ref, slots_ref, out_ref):
    got = jnp.dot(
        merge_ref[...], slots_ref[...].reshape(128, HALF), preferred_element_type=F32
    ).astype(BF16)
    for i in range(8):
        out_ref[i] = got


def merge(table, slots):
    vmem = pl.BlockSpec(memory_space=pltpu.VMEM)
    return pl.pallas_call(
        merge_kernel,
        out_shape=jax.ShapeDtypeStruct((8, LINE_SLOTS, HALF), BF16),
        in_specs=[vmem] * 2,
        out_specs=vmem,
        compiler_params=pltpu.CompilerParams(vmem_limit_bytes=8 << 20),
        name="merge",
    )(table, slots)


def order_kernel(ranks_ref, slots_ref, out_ref):
    row = iota((8 * LINE_SLOTS, NFIT), 0)
    here = ((row >> 6) == ranks_ref[2:3, :]) & ((row & 63) == ranks_ref[1:2, :])
    out_ref[...] = lax.dot_general(
        slots_ref[...].reshape(8 * LINE_SLOTS, HALF),
        jnp.where(here, F32(1.0), F32(0.0)).astype(BF16),
        (((0,), (0,)), ((), ())),
        preferred_element_type=F32,
    ).astype(BF16)


def order(ranks, slots):
    vmem = pl.BlockSpec(memory_space=pltpu.VMEM)
    return pl.pallas_call(
        order_kernel,
        out_shape=jax.ShapeDtypeStruct((HALF, NFIT), BF16),
        in_specs=[vmem] * 2,
        out_specs=vmem,
        compiler_params=pltpu.CompilerParams(vmem_limit_bytes=8 << 20),
        name="order",
    )(ranks, slots)


def any_points(points, orbitals, core, base):
    cell = iota((2048, NFIT), 0) + base
    hot = jnp.where(cell == points, F32(1.0), F32(0.0)).astype(BF16)
    got = jnp.dot(orbitals, hot, preferred_element_type=F32).astype(BF16)
    own = lax.dynamic_slice_in_dim(got, core * HALF, HALF, 0)
    other = lax.dynamic_slice_in_dim(got, (1 - core) * HALF, HALF, 0)
    own = exchange((own + sibling(other)).reshape(N, 8, NFIT), CHIPS)
    own = jnp.sum(own.astype(F32), axis=0).astype(BF16)
    return exchange(jnp.broadcast_to(own[None], (N, 8, NFIT)), CHIPS).reshape(HALF, NFIT)


def hold_kernel(orbitals_ref, held_ref, sem):
    copy = pltpu.make_async_copy(orbitals_ref, held_ref, sem)
    copy.start()
    copy.wait()


def hold(orbitals):
    return pl.pallas_call(
        hold_kernel,
        out_shape=jax.ShapeDtypeStruct(orbitals.shape, orbitals.dtype),
        in_specs=[pl.BlockSpec(memory_space=pltpu.HBM)],
        out_specs=pl.BlockSpec(memory_space=pltpu.VMEM),
        scratch_shapes=[pltpu.SemaphoreType.DMA(())],
        compiler_params=pltpu.CompilerParams(vmem_limit_bytes=8 << 20),
        cost_estimate=pl.CostEstimate(flops=0, bytes_accessed=2**23, transcendentals=0),
        name="hold",
    )(orbitals)


def fit_kernel(core_ref, own_ref, other_ref, table_ref, orbitals_ref, near_ref, far_ref, values_ref):
    core = core_ref[0]
    mine = pl.multiple_of(core * HALF, HALF)
    theirs = pl.multiple_of((1 - core) * HALF, HALF)
    values_ref[pl.ds(mine, HALF), :] = own_ref[...]
    values_ref[pl.ds(theirs, HALF), :] = other_ref[...]
    density = lax.dot_general(
        orbitals_ref[...], values_ref[...], (((0,), (0,)), ((), ())), preferred_element_type=F32
    )
    fitted = (density * density).astype(BF16)
    for j in range(8):
        half_z = jnp.dot(
            table_ref[...], fitted[256 * j : 256 * j + 256], preferred_element_type=F32
        ).astype(BF16)
        near_ref[4 * j : 4 * j + 4] = half_z[:128].reshape(4, 32, NFIT)
        far_ref[4 * j : 4 * j + 4] = half_z[128:].reshape(4, 32, NFIT)


def fit(core, own, other, table, held):
    half = jax.ShapeDtypeStruct((32, 32, NFIT), BF16)
    vmem = pl.BlockSpec(memory_space=pltpu.VMEM)
    return pl.pallas_call(
        fit_kernel,
        out_shape=(half, half),
        in_specs=[pl.BlockSpec(memory_space=pltpu.SMEM)] + [vmem] * 4,
        out_specs=[vmem] * 2,
        scratch_shapes=[pltpu.VMEM((NORB, NFIT), BF16)],
        compiler_params=pltpu.CompilerParams(vmem_limit_bytes=16 << 20),
        name="fit",
    )(core, own, other, table, held)


def y_kernel(core_ref, near_ref, far_ref, table_ref, out_ref, rows_ref):
    core = core_ref[0]
    mine = pl.multiple_of(core * 512, 512)
    theirs = pl.multiple_of((1 - core) * 512, 512)
    for g in range(2):
        rows_ref[pl.ds(mine, 512), :] = near_ref[:, 16 * g : 16 * g + 16, :].reshape(512, NFIT)
        rows_ref[pl.ds(theirs, 512), :] = far_ref[:, 16 * g : 16 * g + 16, :].reshape(512, NFIT)
        for m in range(4):
            got = jnp.dot(
                table_ref[256 * m : 256 * m + 256, :], rows_ref[...], preferred_element_type=F32
            ).astype(BF16)
            out_ref[8 * m : 8 * m + 8, g] = got.reshape(8, 2, 16, NFIT)


def y_transform(core, near, far, table):
    return pl.pallas_call(
        y_kernel,
        out_shape=jax.ShapeDtypeStruct((32, 2, 2, 16, NFIT), BF16),
        in_specs=[pl.BlockSpec(memory_space=pltpu.SMEM)]
        + [pl.BlockSpec(memory_space=pltpu.VMEM)] * 3,
        out_specs=pl.BlockSpec(memory_space=pltpu.VMEM),
        scratch_shapes=[pltpu.VMEM((1024, NFIT), BF16)],
        compiler_params=pltpu.CompilerParams(vmem_limit_bytes=14 << 20),
        name="y_transform",
    )(core, near, far, table)


def gram_kernel(
    core_ref,
    planes_ref,
    table_ref,
    screens_ref,
    mixed_ref,
    own_ref,
    other_ref,
    coeffs_ref,
    weighted_ref,
    screen_ref,
    sem,
):
    copy = pltpu.make_async_copy(screens_ref, screen_ref, sem)
    copy.start()
    mixed = jnp.concatenate([mixed_ref[...]] * 2, axis=1)
    for b in range(2):
        rows = planes_ref[b].reshape(1024, NFIT)
        t0, t1, t2, t3 = [
            jnp.dot(table_ref[256 * t : 256 * t + 256, :], rows, preferred_element_type=F32)
            .astype(BF16)
            .astype(F32)
            for t in range(4)
        ]
        if b == 0:
            copy.wait()
        outs = (t0 - mixed * t3, mixed * t0 + t3, t2 + mixed * t1, mixed * t2 - t1)
        for o, value in enumerate(outs):
            at = slice(256 * o, 256 * o + 256)
            value = value.astype(BF16)
            coeffs_ref[at, 256 * b : 256 * b + 256] = value
            value = value.astype(F32)
            screen = screen_ref[at, :]
            for h in range(2):
                weighted_ref[h, at, 128 * b : 128 * b + 128] = (
                    value[:, 128 * h : 128 * h + 128] * screen
                ).astype(BF16)
    core = core_ref[0]
    for q in range(2):
        left = coeffs_ref[:, 256 * q : 256 * q + 256]
        for half, out_ref in ((core, own_ref), (1 - core, other_ref)):
            got = kernel_scale * lax.dot_general(
                left, weighted_ref[half], (((0,), (0,)), ((), ())), preferred_element_type=F32
            )
            for b in range(2):
                out_ref[b, :, q] = got[:, 128 * b : 128 * b + 128].reshape(32, 8, 128)


def gram(core, planes, table, screen, mixed):
    half = jax.ShapeDtypeStruct((2, 32, 2, 8, 128), F32)
    return pl.pallas_call(
        gram_kernel,
        out_shape=(half, half),
        in_specs=[pl.BlockSpec(memory_space=pltpu.SMEM)]
        + [pl.BlockSpec(memory_space=pltpu.VMEM)] * 2
        + [pl.BlockSpec(memory_space=pltpu.HBM), pl.BlockSpec(memory_space=pltpu.VMEM)],
        out_specs=[pl.BlockSpec(memory_space=pltpu.VMEM)] * 2,
        scratch_shapes=[
            pltpu.VMEM((1024, 512), BF16),
            pltpu.VMEM((2, 1024, 256), BF16),
            pltpu.VMEM((1024, 128), F32),
            pltpu.SemaphoreType.DMA(()),
        ],
        compiler_params=pltpu.CompilerParams(vmem_limit_bytes=20 << 20),
        name="gram",
    )(core, planes, table, screen, mixed)


def sibling(block):
    return lax.ppermute(block, "c", [(0, 1), (1, 0)])


def exchange(blocks, axes):
    return lax.all_to_all(blocks, axes, split_axis=0, concat_axis=0, tiled=True)


def on_device(orbitals, points):
    core = lax.axis_index("c")
    batch = lax.axis_index("b")
    chip = lax.axis_index(CHIPS)
    core_word = core.astype(jnp.int32)[None]
    turn = lax.axis_index(SAME_CORE)
    y_pair, z_group = turn // 4, core * 4 + turn % 4
    base = (chip * 2 + core) * 2048
    place = jnp.stack([core, chip, base]).astype(jnp.int32)
    own, other, ranks, merge_table = pick(place, points, orbitals)
    own = own + sibling(other)
    slots = exchange(jnp.broadcast_to(own[None], (8, CHIP_SLOTS, HALF)), ("z",))

    small = pair_table(iota((N, N), 0), iota((N, N), 1)).astype(BF16)
    z_table, y_big = expand_yz(core_word, small)
    full = (jnp.max(ranks[0]) >= CHIP_SLOTS) | (jnp.max(ranks[1]) >= LINE_SLOTS)
    full = jnp.where(full, F32(1.0), F32(0.0))[None]
    slots, z_table, y_big, full = lax.optimization_barrier((slots, z_table, y_big, full))
    slots = exchange(merge(merge_table, slots), LINES)
    full = full + lax.ppermute(full, "b", [(0, 1), (1, 0)])
    x_small = x_table(y_pair == 0)
    slots, full, orbitals = lax.optimization_barrier((slots, full, orbitals))
    own = order(ranks, slots)
    own = lax.cond(
        full[0] > 0,
        lambda o: any_points(points, orbitals, core, base),
        lambda o: o,
        own,
    )
    held = hold(orbitals)
    near, far = fit(core_word, own, sibling(own), z_table, held)
    x_big = expand_x(x_small)
    screen, mixed = screen_rows(y_pair, z_group * 4)
    screen = pltpu.with_memory_space_constraint(screen, pltpu.HBM)
    planes = y_transform(core_word, near, sibling(far), y_big)
    planes = exchange(planes.reshape(128, 16, NFIT), SAME_CORE).reshape(2, N, 16, NFIT)
    own, other = gram(core_word, planes, x_big, screen, mixed)
    sums = exchange((own + sibling(other)).reshape(128, 8, 128), SAME_CORE)
    sums = jnp.sum(sums, axis=0).reshape(2, 4, 128)
    mine = lax.dynamic_index_in_dim(sums, core, 0, keepdims=False)
    theirs = sibling(lax.dynamic_index_in_dim(sums, 1 - core, 0, keepdims=False))
    pair = jnp.where(core == 0, jnp.stack([mine, theirs]), jnp.stack([theirs, mine]))
    return pair.transpose(0, 2, 1).reshape(NFIT, 4)


def solution(mesh):
    fine = Mesh(mesh.devices.reshape(2, 4, 8, 2, 2), ("yl", "x", "z", "c", "b"))
    grid = ("yl", "x", "z", "c")
    return jax.shard_map(
        on_device,
        mesh=fine,
        in_specs=(P(None, grid), P("b", None)),
        out_specs=P("b", grid),
        check_vma=False,
    )
```

```python
import math

import jax
import jax.numpy as jnp
from jax import lax
from jax.experimental import pallas as pl
from jax.experimental.pallas import tpu as pltpu
from jax.sharding import Mesh
from jax.sharding import PartitionSpec as P

N = 64
NORB = 1024
NFIT = 256
HALF = NORB // 2
CHIP_SLOTS = 16
LINE_SLOTS = 64

screen_rate = 0.05
kernel_scale = 16.0

CHIPS = ("yl", "x", "z")
LINES = ("yl", "x")
SAME_CORE = ("yl", "x", "z", "b")
F32 = jnp.float32
BF16 = jnp.bfloat16


def signed_freq(values):
    return jnp.where(values < N // 2, values, values - N).astype(F32)


def waves(freq, place):
    angles = (freq * place % N).astype(F32) * F32(2.0 * math.pi / N)
    return jnp.cos(angles) / math.sqrt(N), jnp.sin(angles) / math.sqrt(N)


def iota(shape, dim):
    return lax.broadcasted_iota(jnp.int32, shape, dim)


def pair_table(row, place):
    pair, part = row // 2, row % 2
    freq = jnp.where((pair == 0) & (part == 1), N // 2, pair)
    cosine, sine = waves(freq, place)
    return jnp.where((part == 0) | (pair == 0), cosine, -sine)


def x_table(lone):
    row, column = iota((256, 256), 0), iota((256, 256), 1)
    z_of, e, k = row // 128, row // 64 % 2, row % 64
    z_part, y_part, place = column // 128, column // 64 % 2, column % 64
    k_low = k % 32
    turned = (e == 1) & (k_low == 0)
    freq = jnp.where(lone, jnp.where(turned, N // 2, k_low), k)
    cosine, sine = waves(freq, place)
    both = jnp.where(e == y_part, cosine, jnp.where(e == 0, sine, -sine))
    both = jnp.where(z_of == z_part, both, F32(0.0))
    single = jnp.where((e == 0) | turned, cosine, -sine)
    kept = (y_part == k // 32) & (z_part == jnp.where(turned, 1 - z_of, z_of))
    return jnp.where(lone, jnp.where(kept, single, F32(0.0)), both).astype(BF16)


def screen_rows(y_pair, z_first):
    shape = (1024, 128)
    row = iota(shape, 0)
    out, k, z_pair = row // 256, row // 4 % 64, z_first + row % 4
    lone_y, lone_z = y_pair == 0, z_pair == 0
    k_low = k % 32
    edge = lone_y & (k_low == 0)
    second = (out == 1) | (out == 3)
    kx = jnp.where(lone_y, jnp.where(edge & second, N // 2, k_low), k)
    ky = jnp.where(lone_y, jnp.where(k >= 32, N // 2, 0), y_pair)
    z_late = (out == 2) | jnp.where(edge, out == 3, out == 1)
    kz = jnp.where(lone_z, jnp.where(z_late, N // 2, 0), z_pair)
    fx, fy, fz = signed_freq(kx), signed_freq(ky), signed_freq(kz)
    scaled = screen_rate * (fx * fx + fy * fy + fz * fz)
    positive = scaled > 0
    safe = jnp.where(positive, scaled, F32(1.0))
    screen = jnp.where(positive, -jnp.expm1(-safe) / safe, F32(0.0))
    copies = jnp.where(edge & lone_z, F32(1.0), F32(2.0))
    mixed = jnp.where(lone_z | edge, F32(0.0), F32(1.0))[:256]
    return screen * copies, mixed


def spread(small, row_of, column_of, first, rows, columns):
    r = first + iota((rows, small.shape[0]), 0)
    c = iota((small.shape[1], columns), 1)
    left = jnp.where(row_of(r) == iota(r.shape, 1), F32(1.0), F32(0.0)).astype(BF16)
    right = jnp.where(column_of(c) == iota(c.shape, 0), F32(1.0), F32(0.0)).astype(BF16)
    tall = jnp.dot(left, small, preferred_element_type=F32).astype(BF16)
    return jnp.dot(tall, right, preferred_element_type=F32)


def expand_yz_kernel(core_ref, small_ref, z_ref, y_ref):
    core = core_ref[0]
    small = small_ref[...]
    row, column = iota((256, 256), 0), iota((256, 256), 1)
    wide = spread(
        small,
        lambda r: jnp.where(r < 128, core, 1 - core) * 32 + (r & 31),
        lambda c: c & 63,
        0,
        256,
        256,
    )
    same = ((row >> 5) & 3) == (column >> 6)
    z_ref[...] = jnp.where(same, wide, F32(0.0)).astype(BF16)
    column = iota((256, 1024), 1)
    for block in range(4):
        row = 256 * block + iota((256, 1024), 0)
        wide = spread(
            small, lambda r: (r >> 5) * 2 + ((r >> 3) & 1), lambda c: c >> 4, 256 * block, 256, 1024
        )
        same = (((row >> 4) & 1) == ((column >> 3) & 1)) & ((row & 7) == (column & 7))
        y_ref[256 * block : 256 * block + 256, :] = jnp.where(same, wide, F32(0.0)).astype(BF16)


def expand_yz(core, small):
    vmem = pl.BlockSpec(memory_space=pltpu.VMEM)
    return pl.pallas_call(
        expand_yz_kernel,
        out_shape=(
            jax.ShapeDtypeStruct((256, 256), BF16),
            jax.ShapeDtypeStruct((1024, 1024), BF16),
        ),
        in_specs=[pl.BlockSpec(memory_space=pltpu.SMEM), vmem],
        out_specs=[vmem] * 2,
        compiler_params=pltpu.CompilerParams(vmem_limit_bytes=16 << 20),
        cost_estimate=pl.CostEstimate(flops=2**30, bytes_accessed=2**21, transcendentals=0),
        name="expand_yz",
    )(core, small)


def expand_x_kernel(small_ref, x_ref):
    column = iota((256, 1024), 1)
    for block in range(4):
        row = 256 * block + iota((256, 1024), 0)
        wide = spread(
            small_ref[...],
            lambda r: r >> 2,
            lambda c: (c & 1) * 128 + ((c >> 3) & 1) * 64 + (c >> 4),
            256 * block,
            256,
            1024,
        )
        same = (row & 3) == ((column >> 1) & 3)
        x_ref[256 * block : 256 * block + 256, :] = jnp.where(same, wide, F32(0.0)).astype(BF16)


def expand_x(small):
    vmem = pl.BlockSpec(memory_space=pltpu.VMEM)
    return pl.pallas_call(
        expand_x_kernel,
        out_shape=jax.ShapeDtypeStruct((1024, 1024), BF16),
        in_specs=[vmem],
        out_specs=vmem,
        compiler_params=pltpu.CompilerParams(vmem_limit_bytes=16 << 20),
        cost_estimate=pl.CostEstimate(flops=2**31, bytes_accessed=2**21, transcendentals=0),
        name="expand_x",
    )(small)


def pick_kernel(
    place_ref, points_ref, orbitals_ref, own_ref, other_ref, ranks_ref, merge_ref, held_ref, got_ref, sem
):
    copy = pltpu.make_async_copy(orbitals_ref, held_ref, sem)
    copy.start()
    core, chip, base = place_ref[0], place_ref[1], place_ref[2]
    points = points_ref[...]
    columns = jnp.broadcast_to(points.astype(F32), (128, NFIT)).T.astype(jnp.int32)
    column = jnp.concatenate([columns] * 2, axis=1)
    before_row = iota((NFIT, NFIT), 0) < iota((NFIT, NFIT), 1)
    before_column = iota((NFIT, NFIT), 1) < iota((NFIT, NFIT), 0)

    def count(matches, axis):
        return jnp.sum(jnp.where(matches, F32(1.0), F32(0.0)), axis=axis, keepdims=True)

    same_chip = (column >> 12) == (points >> 12)
    same_line = (column >> 15) == (points >> 15)
    chip_rank = count(same_chip & before_row, 0).astype(jnp.int32)
    line_rank = count(same_line & before_row, 0).astype(jnp.int32)
    rank_column = count(same_chip & before_column, 1).astype(jnp.int32)
    ranks_ref[0:1, :] = chip_rank
    ranks_ref[1:2, :] = line_rank
    ranks_ref[2:3, :] = points >> 15

    slot = iota((NFIT, 128), 1)
    chosen = ((columns >> 12) == chip) & (rank_column == slot)
    offsets = jnp.max(
        jnp.where(chosen, (columns - base).astype(F32), F32(-1.0)), axis=0, keepdims=True
    ).astype(jnp.int32)
    hot = jnp.where(iota((2048, 128), 0) == offsets, F32(1.0), F32(0.0)).astype(BF16)

    to_slot = ((points >> 15) == (chip >> 3)) & (line_rank == iota((LINE_SLOTS, NFIT), 0))
    from_slot = (((columns >> 12) & 7) == (slot >> 4)) & (rank_column == (slot & 15))
    merge_ref[...] = jnp.dot(
        jnp.where(to_slot, F32(1.0), F32(0.0)).astype(BF16),
        jnp.where(from_slot, F32(1.0), F32(0.0)).astype(BF16),
        preferred_element_type=F32,
    ).astype(BF16)

    copy.wait()
    got = jnp.dot(held_ref[...], hot, preferred_element_type=F32)
    got_ref[...] = got.T[:CHIP_SLOTS].astype(BF16)
    own_ref[...] = got_ref[:, pl.ds(pl.multiple_of(core * HALF, HALF), HALF)]
    other_ref[...] = got_ref[:, pl.ds(pl.multiple_of((1 - core) * HALF, HALF), HALF)]


def pick(place, points, orbitals):
    half = jax.ShapeDtypeStruct((CHIP_SLOTS, HALF), BF16)
    vmem = pl.BlockSpec(memory_space=pltpu.VMEM)
    return pl.pallas_call(
        pick_kernel,
        out_shape=(
            half,
            half,
            jax.ShapeDtypeStruct((8, NFIT), jnp.int32),
            jax.ShapeDtypeStruct((LINE_SLOTS, 128), BF16),
        ),
        in_specs=[pl.BlockSpec(memory_space=pltpu.SMEM), vmem, pl.BlockSpec(memory_space=pltpu.HBM)],
        out_specs=[vmem] * 4,
        scratch_shapes=[
            pltpu.VMEM((NORB, 2048), BF16),
            pltpu.VMEM((CHIP_SLOTS, NORB), BF16),
            pltpu.SemaphoreType.DMA(()),
        ],
        compiler_params=pltpu.CompilerParams(vmem_limit_bytes=16 << 20),
        name="pick",
    )(place, points, orbitals)


def merge_kernel(merge_ref, slots_ref, out_ref):
    got = jnp.dot(
        merge_ref[...], slots_ref[...].reshape(128, HALF), preferred_element_type=F32
    ).astype(BF16)
    for i in range(8):
        out_ref[i] = got


def merge(table, slots):
    vmem = pl.BlockSpec(memory_space=pltpu.VMEM)
    return pl.pallas_call(
        merge_kernel,
        out_shape=jax.ShapeDtypeStruct((8, LINE_SLOTS, HALF), BF16),
        in_specs=[vmem] * 2,
        out_specs=vmem,
        compiler_params=pltpu.CompilerParams(vmem_limit_bytes=8 << 20),
        name="merge",
    )(table, slots)


def order_kernel(ranks_ref, slots_ref, out_ref):
    row = iota((8 * LINE_SLOTS, NFIT), 0)
    here = ((row >> 6) == ranks_ref[2:3, :]) & ((row & 63) == ranks_ref[1:2, :])
    out_ref[...] = lax.dot_general(
        slots_ref[...].reshape(8 * LINE_SLOTS, HALF),
        jnp.where(here, F32(1.0), F32(0.0)).astype(BF16),
        (((0,), (0,)), ((), ())),
        preferred_element_type=F32,
    ).astype(BF16)


def order(ranks, slots):
    vmem = pl.BlockSpec(memory_space=pltpu.VMEM)
    return pl.pallas_call(
        order_kernel,
        out_shape=jax.ShapeDtypeStruct((HALF, NFIT), BF16),
        in_specs=[vmem] * 2,
        out_specs=vmem,
        compiler_params=pltpu.CompilerParams(vmem_limit_bytes=8 << 20),
        name="order",
    )(ranks, slots)


def any_points(points, orbitals, core, base):
    cell = iota((2048, NFIT), 0) + base
    hot = jnp.where(cell == points, F32(1.0), F32(0.0)).astype(BF16)
    got = jnp.dot(orbitals, hot, preferred_element_type=F32).astype(BF16)
    own = lax.dynamic_slice_in_dim(got, core * HALF, HALF, 0)
    other = lax.dynamic_slice_in_dim(got, (1 - core) * HALF, HALF, 0)
    own = exchange((own + sibling(other)).reshape(N, 8, NFIT), CHIPS)
    own = jnp.sum(own.astype(F32), axis=0).astype(BF16)
    return exchange(jnp.broadcast_to(own[None], (N, 8, NFIT)), CHIPS).reshape(HALF, NFIT)


def hold_kernel(orbitals_ref, held_ref, sem):
    copy = pltpu.make_async_copy(orbitals_ref, held_ref, sem)
    copy.start()
    copy.wait()


def hold(orbitals):
    return pl.pallas_call(
        hold_kernel,
        out_shape=jax.ShapeDtypeStruct(orbitals.shape, orbitals.dtype),
        in_specs=[pl.BlockSpec(memory_space=pltpu.HBM)],
        out_specs=pl.BlockSpec(memory_space=pltpu.VMEM),
        scratch_shapes=[pltpu.SemaphoreType.DMA(())],
        compiler_params=pltpu.CompilerParams(vmem_limit_bytes=8 << 20),
        cost_estimate=pl.CostEstimate(flops=0, bytes_accessed=2**23, transcendentals=0),
        name="hold",
    )(orbitals)


def fit_kernel(core_ref, own_ref, other_ref, table_ref, orbitals_ref, near_ref, far_ref, values_ref):
    core = core_ref[0]
    mine = pl.multiple_of(core * HALF, HALF)
    theirs = pl.multiple_of((1 - core) * HALF, HALF)
    values_ref[pl.ds(mine, HALF), :] = own_ref[...]
    values_ref[pl.ds(theirs, HALF), :] = other_ref[...]
    density = lax.dot_general(
        orbitals_ref[...], values_ref[...], (((0,), (0,)), ((), ())), preferred_element_type=F32
    )
    fitted = (density * density).astype(BF16)
    for j in range(8):
        half_z = jnp.dot(
            table_ref[...], fitted[256 * j : 256 * j + 256], preferred_element_type=F32
        ).astype(BF16)
        near_ref[4 * j : 4 * j + 4] = half_z[:128].reshape(4, 32, NFIT)
        far_ref[4 * j : 4 * j + 4] = half_z[128:].reshape(4, 32, NFIT)


def fit(core, own, other, table, held):
    half = jax.ShapeDtypeStruct((32, 32, NFIT), BF16)
    vmem = pl.BlockSpec(memory_space=pltpu.VMEM)
    return pl.pallas_call(
        fit_kernel,
        out_shape=(half, half),
        in_specs=[pl.BlockSpec(memory_space=pltpu.SMEM)] + [vmem] * 4,
        out_specs=[vmem] * 2,
        scratch_shapes=[pltpu.VMEM((NORB, NFIT), BF16)],
        compiler_params=pltpu.CompilerParams(vmem_limit_bytes=16 << 20),
        name="fit",
    )(core, own, other, table, held)


def y_near_kernel(core_ref, near_ref, table_ref, part_ref):
    at = pl.ds(pl.multiple_of(core_ref[0] * 512, 512), 512)
    for g in range(2):
        rows = near_ref[:, 16 * g : 16 * g + 16, :].reshape(512, NFIT)
        part_ref[g] = jnp.dot(table_ref[:, at], rows, preferred_element_type=F32)


def y_near(core, near, table):
    vmem = pl.BlockSpec(memory_space=pltpu.VMEM)
    return pl.pallas_call(
        y_near_kernel,
        out_shape=jax.ShapeDtypeStruct((2, 1024, NFIT), F32),
        in_specs=[pl.BlockSpec(memory_space=pltpu.SMEM)] + [vmem] * 2,
        out_specs=vmem,
        compiler_params=pltpu.CompilerParams(vmem_limit_bytes=12 << 20),
        cost_estimate=pl.CostEstimate(flops=2**29, bytes_accessed=2**22, transcendentals=0),
        name="y_near",
    )(core, near, table)


def y_far_kernel(core_ref, far_ref, table_ref, part_ref, out_ref):
    at = pl.ds(pl.multiple_of((1 - core_ref[0]) * 512, 512), 512)
    for g in range(2):
        rows = far_ref[:, 16 * g : 16 * g + 16, :].reshape(512, NFIT)
        got = part_ref[g] + jnp.dot(table_ref[:, at], rows, preferred_element_type=F32)
        out_ref[:, g] = got.astype(BF16).reshape(32, 2, 16, NFIT)


def y_far(core, far, table, part):
    vmem = pl.BlockSpec(memory_space=pltpu.VMEM)
    return pl.pallas_call(
        y_far_kernel,
        out_shape=jax.ShapeDtypeStruct((32, 2, 2, 16, NFIT), BF16),
        in_specs=[pl.BlockSpec(memory_space=pltpu.SMEM)] + [vmem] * 3,
        out_specs=vmem,
        compiler_params=pltpu.CompilerParams(vmem_limit_bytes=14 << 20),
        name="y_far",
    )(core, far, table, part)


def gram_kernel(
    core_ref,
    planes_ref,
    table_ref,
    screens_ref,
    mixed_ref,
    own_ref,
    other_ref,
    coeffs_ref,
    weighted_ref,
    screen_ref,
    sem,
):
    copy = pltpu.make_async_copy(screens_ref, screen_ref, sem)
    copy.start()
    mixed = jnp.concatenate([mixed_ref[...]] * 2, axis=1)
    for b in range(2):
        rows = planes_ref[:, b].reshape(1024, NFIT)
        t0, t1, t2, t3 = [
            jnp.dot(table_ref[256 * t : 256 * t + 256, :], rows, preferred_element_type=F32)
            .astype(BF16)
            .astype(F32)
            for t in range(4)
        ]
        if b == 0:
            copy.wait()
        outs = (t0 - mixed * t3, mixed * t0 + t3, t2 + mixed * t1, mixed * t2 - t1)
        for o, value in enumerate(outs):
            at = slice(256 * o, 256 * o + 256)
            value = value.astype(BF16)
            coeffs_ref[at, 256 * b : 256 * b + 256] = value
            value = value.astype(F32)
            screen = screen_ref[at, :]
            for h in range(2):
                weighted_ref[h, at, 128 * b : 128 * b + 128] = (
                    value[:, 128 * h : 128 * h + 128] * screen
                ).astype(BF16)
    core = core_ref[0]
    for q in range(2):
        left = coeffs_ref[:, 256 * q : 256 * q + 256]
        for half, out_ref in ((core, own_ref), (1 - core, other_ref)):
            got = kernel_scale * lax.dot_general(
                left, weighted_ref[half], (((0,), (0,)), ((), ())), preferred_element_type=F32
            )
            for b in range(2):
                out_ref[32 * q : 32 * q + 32, b] = got[:, 128 * b : 128 * b + 128].reshape(32, 8, 128)


def gram(core, planes, table, screen, mixed):
    half = jax.ShapeDtypeStruct((N, 2, 8, 128), F32)
    return pl.pallas_call(
        gram_kernel,
        out_shape=(half, half),
        in_specs=[pl.BlockSpec(memory_space=pltpu.SMEM)]
        + [pl.BlockSpec(memory_space=pltpu.VMEM)] * 2
        + [pl.BlockSpec(memory_space=pltpu.HBM), pl.BlockSpec(memory_space=pltpu.VMEM)],
        out_specs=[pl.BlockSpec(memory_space=pltpu.VMEM)] * 2,
        scratch_shapes=[
            pltpu.VMEM((1024, 512), BF16),
            pltpu.VMEM((2, 1024, 256), BF16),
            pltpu.VMEM((1024, 128), F32),
            pltpu.SemaphoreType.DMA(()),
        ],
        compiler_params=pltpu.CompilerParams(vmem_limit_bytes=20 << 20),
        name="gram",
    )(core, planes, table, screen, mixed)


def sibling(block):
    return lax.ppermute(block, "c", [(0, 1), (1, 0)])


def exchange(blocks, axes):
    return lax.all_to_all(blocks, axes, split_axis=0, concat_axis=0, tiled=True)


def on_device(orbitals, points):
    core = lax.axis_index("c")
    batch = lax.axis_index("b")
    chip = lax.axis_index(CHIPS)
    core_word = core.astype(jnp.int32)[None]
    y_pair, z_group = chip // 2, core * 4 + chip % 2 * 2 + batch
    base = (chip * 2 + core) * 2048
    place = jnp.stack([core, chip, base]).astype(jnp.int32)
    own, other, ranks, merge_table = pick(place, points, orbitals)
    own = own + sibling(other)
    slots = exchange(jnp.broadcast_to(own[None], (8, CHIP_SLOTS, HALF)), ("z",))

    small = pair_table(iota((N, N), 0), iota((N, N), 1)).astype(BF16)
    z_table, y_big = expand_yz(core_word, small)
    full = (jnp.max(ranks[0]) >= CHIP_SLOTS) | (jnp.max(ranks[1]) >= LINE_SLOTS)
    full = jnp.where(full, F32(1.0), F32(0.0))[None]
    full = full + lax.ppermute(full, "b", [(0, 1), (1, 0)])
    slots, full = lax.optimization_barrier((slots, full))
    slots = exchange(merge(merge_table, slots), LINES)
    slots, z_table, y_big, orbitals = lax.optimization_barrier((slots, z_table, y_big, orbitals))
    own = order(ranks, slots)
    own = lax.cond(
        full[0] > 0,
        lambda o: any_points(points, orbitals, core, base),
        lambda o: o,
        own,
    )
    held = hold(orbitals)
    near, far = fit(core_word, own, sibling(own), z_table, held)
    x_big = expand_x(x_table(y_pair == 0))
    screen, mixed = screen_rows(y_pair, z_group * 4)
    screen = pltpu.with_memory_space_constraint(screen, pltpu.HBM)
    planes = y_far(core_word, sibling(far), y_big, y_near(core_word, near, y_big))
    planes = exchange(planes.reshape(128, 16, NFIT), SAME_CORE).reshape(N, 2, 16, NFIT)
    own, other = gram(core_word, planes, x_big, screen, mixed)
    sums = exchange((own + sibling(other)).reshape(128, 8, 128), SAME_CORE)
    sums = jnp.sum(sums, axis=0).reshape(2, 4, 128)
    mine = lax.dynamic_index_in_dim(sums, core, 0, keepdims=False)
    theirs = sibling(lax.dynamic_index_in_dim(sums, 1 - core, 0, keepdims=False))
    pair = jnp.where(core == 0, jnp.stack([mine, theirs]), jnp.stack([theirs, mine]))
    return pair.transpose(0, 2, 1).reshape(NFIT, 4)


def solution(mesh):
    fine = Mesh(mesh.devices.reshape(2, 4, 8, 2, 2), ("yl", "x", "z", "c", "b"))
    grid = ("yl", "x", "z", "c")
    return jax.shard_map(
        on_device,
        mesh=fine,
        in_specs=(P(None, grid), P("b", None)),
        out_specs=P("b", grid),
        check_vma=False,
    )
```

```python
import math

import jax
import jax.numpy as jnp
from jax import lax
from jax.experimental import pallas as pl
from jax.experimental.pallas import tpu as pltpu
from jax.sharding import Mesh
from jax.sharding import PartitionSpec as P

N = 64
NORB = 1024
NFIT = 256
HALF = NORB // 2
CHIP_SLOTS = 16
LINE_SLOTS = 64

screen_rate = 0.05
kernel_scale = 16.0

CHIPS = ("yl", "x", "z")
LINES = ("yl", "x")
SAME_CORE = ("yl", "x", "z", "b")
F32 = jnp.float32
BF16 = jnp.bfloat16


def signed_freq(values):
    return jnp.where(values < N // 2, values, values - N).astype(F32)


def waves(freq, place):
    angles = (freq * place % N).astype(F32) * F32(2.0 * math.pi / N)
    return jnp.cos(angles) / math.sqrt(N), jnp.sin(angles) / math.sqrt(N)


def iota(shape, dim):
    return lax.broadcasted_iota(jnp.int32, shape, dim)


def pair_table(row, place):
    pair, part = row // 2, row % 2
    freq = jnp.where((pair == 0) & (part == 1), N // 2, pair)
    cosine, sine = waves(freq, place)
    return jnp.where((part == 0) | (pair == 0), cosine, -sine)


def x_table(lone):
    row, column = iota((256, 256), 0), iota((256, 256), 1)
    z_of, e, k = row // 128, row // 64 % 2, row % 64
    z_part, y_part, place = column // 128, column // 64 % 2, column % 64
    k_low = k % 32
    turned = (e == 1) & (k_low == 0)
    freq = jnp.where(lone, jnp.where(turned, N // 2, k_low), k)
    cosine, sine = waves(freq, place)
    both = jnp.where(e == y_part, cosine, jnp.where(e == 0, sine, -sine))
    both = jnp.where(z_of == z_part, both, F32(0.0))
    single = jnp.where((e == 0) | turned, cosine, -sine)
    kept = (y_part == k // 32) & (z_part == jnp.where(turned, 1 - z_of, z_of))
    return jnp.where(lone, jnp.where(kept, single, F32(0.0)), both).astype(BF16)


def screen_rows(y_pair, z_first):
    shape = (1024, 128)
    row = iota(shape, 0)
    out, k, z_pair = row // 256, row // 4 % 64, z_first + row % 4
    lone_y, lone_z = y_pair == 0, z_pair == 0
    k_low = k % 32
    edge = lone_y & (k_low == 0)
    second = (out == 1) | (out == 3)
    kx = jnp.where(lone_y, jnp.where(edge & second, N // 2, k_low), k)
    ky = jnp.where(lone_y, jnp.where(k >= 32, N // 2, 0), y_pair)
    z_late = (out == 2) | jnp.where(edge, out == 3, out == 1)
    kz = jnp.where(lone_z, jnp.where(z_late, N // 2, 0), z_pair)
    fx, fy, fz = signed_freq(kx), signed_freq(ky), signed_freq(kz)
    scaled = screen_rate * (fx * fx + fy * fy + fz * fz)
    positive = scaled > 0
    safe = jnp.where(positive, scaled, F32(1.0))
    screen = jnp.where(positive, -jnp.expm1(-safe) / safe, F32(0.0))
    copies = jnp.where(edge & lone_z, F32(1.0), F32(2.0))
    mixed = jnp.where(lone_z | edge, F32(0.0), F32(1.0))[:256]
    return screen * copies, mixed


def spread(small, row_of, column_of, first, rows, columns):
    r = first + iota((rows, small.shape[0]), 0)
    c = iota((small.shape[1], columns), 1)
    left = jnp.where(row_of(r) == iota(r.shape, 1), F32(1.0), F32(0.0)).astype(BF16)
    right = jnp.where(column_of(c) == iota(c.shape, 0), F32(1.0), F32(0.0)).astype(BF16)
    tall = jnp.dot(left, small, preferred_element_type=F32).astype(BF16)
    return jnp.dot(tall, right, preferred_element_type=F32)


def expand_yz_kernel(core_ref, small_ref, z_ref, y_ref):
    core = core_ref[0]
    small = small_ref[...]
    row, column = iota((256, 256), 0), iota((256, 256), 1)
    wide = spread(
        small,
        lambda r: jnp.where(r < 128, core, 1 - core) * 32 + (r & 31),
        lambda c: c & 63,
        0,
        256,
        256,
    )
    same = ((row >> 5) & 3) == (column >> 6)
    z_ref[...] = jnp.where(same, wide, F32(0.0)).astype(BF16)
    column = iota((256, 1024), 1)
    for block in range(4):
        row = 256 * block + iota((256, 1024), 0)
        wide = spread(
            small, lambda r: (r >> 5) * 2 + ((r >> 3) & 1), lambda c: c >> 4, 256 * block, 256, 1024
        )
        same = (((row >> 4) & 1) == ((column >> 3) & 1)) & ((row & 7) == (column & 7))
        y_ref[256 * block : 256 * block + 256, :] = jnp.where(same, wide, F32(0.0)).astype(BF16)


def expand_yz(core, small):
    vmem = pl.BlockSpec(memory_space=pltpu.VMEM)
    return pl.pallas_call(
        expand_yz_kernel,
        out_shape=(
            jax.ShapeDtypeStruct((256, 256), BF16),
            jax.ShapeDtypeStruct((1024, 1024), BF16),
        ),
        in_specs=[pl.BlockSpec(memory_space=pltpu.SMEM), vmem],
        out_specs=[vmem] * 2,
        compiler_params=pltpu.CompilerParams(vmem_limit_bytes=16 << 20),
        cost_estimate=pl.CostEstimate(flops=2**30, bytes_accessed=2**21, transcendentals=0),
        name="expand_yz",
    )(core, small)


def expand_x_kernel(small_ref, x_ref):
    column = iota((256, 1024), 1)
    for block in range(4):
        row = 256 * block + iota((256, 1024), 0)
        wide = spread(
            small_ref[...],
            lambda r: r >> 2,
            lambda c: (c & 1) * 128 + ((c >> 3) & 1) * 64 + (c >> 4),
            256 * block,
            256,
            1024,
        )
        same = (row & 3) == ((column >> 1) & 3)
        x_ref[256 * block : 256 * block + 256, :] = jnp.where(same, wide, F32(0.0)).astype(BF16)


def expand_x(small):
    vmem = pl.BlockSpec(memory_space=pltpu.VMEM)
    return pl.pallas_call(
        expand_x_kernel,
        out_shape=jax.ShapeDtypeStruct((1024, 1024), BF16),
        in_specs=[vmem],
        out_specs=vmem,
        compiler_params=pltpu.CompilerParams(vmem_limit_bytes=16 << 20),
        cost_estimate=pl.CostEstimate(flops=2**31, bytes_accessed=2**21, transcendentals=0),
        name="expand_x",
    )(small)


def pick_kernel(
    place_ref, points_ref, orbitals_ref, own_ref, other_ref, ranks_ref, merge_ref, held_ref, got_ref, sem
):
    copy = pltpu.make_async_copy(orbitals_ref, held_ref, sem)
    copy.start()
    core, chip, base = place_ref[0], place_ref[1], place_ref[2]
    points = points_ref[...]
    columns = jnp.broadcast_to(points.astype(F32), (128, NFIT)).T.astype(jnp.int32)
    column = jnp.concatenate([columns] * 2, axis=1)
    before_row = iota((NFIT, NFIT), 0) < iota((NFIT, NFIT), 1)
    before_column = iota((NFIT, NFIT), 1) < iota((NFIT, NFIT), 0)

    def count(matches, axis):
        return jnp.sum(jnp.where(matches, F32(1.0), F32(0.0)), axis=axis, keepdims=True)

    same_chip = (column >> 12) == (points >> 12)
    same_line = (column >> 15) == (points >> 15)
    chip_rank = count(same_chip & before_row, 0).astype(jnp.int32)
    line_rank = count(same_line & before_row, 0).astype(jnp.int32)
    rank_column = count(same_chip & before_column, 1).astype(jnp.int32)
    ranks_ref[0:1, :] = chip_rank
    ranks_ref[1:2, :] = line_rank
    ranks_ref[2:3, :] = points >> 15

    slot = iota((NFIT, 128), 1)
    chosen = ((columns >> 12) == chip) & (rank_column == slot)
    offsets = jnp.max(
        jnp.where(chosen, (columns - base).astype(F32), F32(-1.0)), axis=0, keepdims=True
    ).astype(jnp.int32)
    hot = jnp.where(iota((2048, 128), 0) == offsets, F32(1.0), F32(0.0)).astype(BF16)

    to_slot = ((points >> 15) == (chip >> 3)) & (line_rank == iota((LINE_SLOTS, NFIT), 0))
    from_slot = (((columns >> 12) & 7) == (slot >> 4)) & (rank_column == (slot & 15))
    merge_ref[...] = jnp.dot(
        jnp.where(to_slot, F32(1.0), F32(0.0)).astype(BF16),
        jnp.where(from_slot, F32(1.0), F32(0.0)).astype(BF16),
        preferred_element_type=F32,
    ).astype(BF16)

    copy.wait()
    got = jnp.dot(held_ref[...], hot, preferred_element_type=F32)
    got_ref[...] = got.T[:CHIP_SLOTS].astype(BF16)
    own_ref[...] = got_ref[:, pl.ds(pl.multiple_of(core * HALF, HALF), HALF)]
    other_ref[...] = got_ref[:, pl.ds(pl.multiple_of((1 - core) * HALF, HALF), HALF)]


def pick(place, points, orbitals):
    half = jax.ShapeDtypeStruct((CHIP_SLOTS, HALF), BF16)
    vmem = pl.BlockSpec(memory_space=pltpu.VMEM)
    return pl.pallas_call(
        pick_kernel,
        out_shape=(
            half,
            half,
            jax.ShapeDtypeStruct((8, NFIT), jnp.int32),
            jax.ShapeDtypeStruct((LINE_SLOTS, 128), BF16),
        ),
        in_specs=[pl.BlockSpec(memory_space=pltpu.SMEM), vmem, pl.BlockSpec(memory_space=pltpu.HBM)],
        out_specs=[vmem] * 4,
        scratch_shapes=[
            pltpu.VMEM((NORB, 2048), BF16),
            pltpu.VMEM((CHIP_SLOTS, NORB), BF16),
            pltpu.SemaphoreType.DMA(()),
        ],
        compiler_params=pltpu.CompilerParams(vmem_limit_bytes=16 << 20),
        name="pick",
    )(place, points, orbitals)


def merge_kernel(merge_ref, slots_ref, out_ref):
    got = jnp.dot(
        merge_ref[...], slots_ref[...].reshape(128, HALF), preferred_element_type=F32
    ).astype(BF16)
    for i in range(8):
        out_ref[i] = got


def merge(table, slots):
    vmem = pl.BlockSpec(memory_space=pltpu.VMEM)
    return pl.pallas_call(
        merge_kernel,
        out_shape=jax.ShapeDtypeStruct((8, LINE_SLOTS, HALF), BF16),
        in_specs=[vmem] * 2,
        out_specs=vmem,
        compiler_params=pltpu.CompilerParams(vmem_limit_bytes=8 << 20),
        name="merge",
    )(table, slots)


def order_kernel(ranks_ref, slots_ref, out_ref):
    row = iota((8 * LINE_SLOTS, NFIT), 0)
    here = ((row >> 6) == ranks_ref[2:3, :]) & ((row & 63) == ranks_ref[1:2, :])
    out_ref[...] = lax.dot_general(
        slots_ref[...].reshape(8 * LINE_SLOTS, HALF),
        jnp.where(here, F32(1.0), F32(0.0)).astype(BF16),
        (((0,), (0,)), ((), ())),
        preferred_element_type=F32,
    ).astype(BF16)


def order(ranks, slots):
    vmem = pl.BlockSpec(memory_space=pltpu.VMEM)
    return pl.pallas_call(
        order_kernel,
        out_shape=jax.ShapeDtypeStruct((HALF, NFIT), BF16),
        in_specs=[vmem] * 2,
        out_specs=vmem,
        compiler_params=pltpu.CompilerParams(vmem_limit_bytes=8 << 20),
        name="order",
    )(ranks, slots)


def any_points(points, orbitals, core, base):
    cell = iota((2048, NFIT), 0) + base
    hot = jnp.where(cell == points, F32(1.0), F32(0.0)).astype(BF16)
    got = jnp.dot(orbitals, hot, preferred_element_type=F32).astype(BF16)
    own = lax.dynamic_slice_in_dim(got, core * HALF, HALF, 0)
    other = lax.dynamic_slice_in_dim(got, (1 - core) * HALF, HALF, 0)
    own = exchange((own + sibling(other)).reshape(N, 8, NFIT), CHIPS)
    own = jnp.sum(own.astype(F32), axis=0).astype(BF16)
    return exchange(jnp.broadcast_to(own[None], (N, 8, NFIT)), CHIPS).reshape(HALF, NFIT)


def hold_kernel(orbitals_ref, held_ref, sem):
    copy = pltpu.make_async_copy(orbitals_ref, held_ref, sem)
    copy.start()
    copy.wait()


def hold(orbitals):
    return pl.pallas_call(
        hold_kernel,
        out_shape=jax.ShapeDtypeStruct(orbitals.shape, orbitals.dtype),
        in_specs=[pl.BlockSpec(memory_space=pltpu.HBM)],
        out_specs=pl.BlockSpec(memory_space=pltpu.VMEM),
        scratch_shapes=[pltpu.SemaphoreType.DMA(())],
        compiler_params=pltpu.CompilerParams(vmem_limit_bytes=8 << 20),
        cost_estimate=pl.CostEstimate(flops=0, bytes_accessed=2**23, transcendentals=0),
        name="hold",
    )(orbitals)


def fit_kernel(core_ref, own_ref, other_ref, table_ref, orbitals_ref, near_ref, far_ref, values_ref):
    core = core_ref[0]
    mine = pl.multiple_of(core * HALF, HALF)
    theirs = pl.multiple_of((1 - core) * HALF, HALF)
    values_ref[pl.ds(mine, HALF), :] = own_ref[...]
    values_ref[pl.ds(theirs, HALF), :] = other_ref[...]
    density = lax.dot_general(
        orbitals_ref[...], values_ref[...], (((0,), (0,)), ((), ())), preferred_element_type=F32
    )
    fitted = (density * density).astype(BF16)
    for j in range(8):
        half_z = jnp.dot(
            table_ref[...], fitted[256 * j : 256 * j + 256], preferred_element_type=F32
        ).astype(BF16)
        near_ref[4 * j : 4 * j + 4] = half_z[:128].reshape(4, 32, NFIT)
        far_ref[4 * j : 4 * j + 4] = half_z[128:].reshape(4, 32, NFIT)


def fit(core, own, other, table, held):
    half = jax.ShapeDtypeStruct((32, 32, NFIT), BF16)
    vmem = pl.BlockSpec(memory_space=pltpu.VMEM)
    return pl.pallas_call(
        fit_kernel,
        out_shape=(half, half),
        in_specs=[pl.BlockSpec(memory_space=pltpu.SMEM)] + [vmem] * 4,
        out_specs=[vmem] * 2,
        scratch_shapes=[pltpu.VMEM((NORB, NFIT), BF16)],
        compiler_params=pltpu.CompilerParams(vmem_limit_bytes=16 << 20),
        name="fit",
    )(core, own, other, table, held)


def y_near_kernel(core_ref, near_ref, table_ref, part_ref):
    at = pl.ds(pl.multiple_of(core_ref[0] * 512, 512), 512)
    for g in range(2):
        rows = near_ref[:, 16 * g : 16 * g + 16, :].reshape(512, NFIT)
        part_ref[g] = jnp.dot(table_ref[:, at], rows, preferred_element_type=F32)


def y_near(core, near, table):
    vmem = pl.BlockSpec(memory_space=pltpu.VMEM)
    return pl.pallas_call(
        y_near_kernel,
        out_shape=jax.ShapeDtypeStruct((2, 1024, NFIT), F32),
        in_specs=[pl.BlockSpec(memory_space=pltpu.SMEM)] + [vmem] * 2,
        out_specs=vmem,
        compiler_params=pltpu.CompilerParams(vmem_limit_bytes=12 << 20),
        cost_estimate=pl.CostEstimate(flops=2**29, bytes_accessed=2**22, transcendentals=0),
        name="y_near",
    )(core, near, table)


def y_far_kernel(core_ref, far_ref, table_ref, part_ref, out_ref):
    at = pl.ds(pl.multiple_of((1 - core_ref[0]) * 512, 512), 512)
    for g in range(2):
        rows = far_ref[:, 16 * g : 16 * g + 16, :].reshape(512, NFIT)
        got = part_ref[g] + jnp.dot(table_ref[:, at], rows, preferred_element_type=F32)
        out_ref[:, g] = got.astype(BF16).reshape(32, 2, 16, NFIT)


def y_far(core, far, table, part):
    vmem = pl.BlockSpec(memory_space=pltpu.VMEM)
    return pl.pallas_call(
        y_far_kernel,
        out_shape=jax.ShapeDtypeStruct((32, 2, 2, 16, NFIT), BF16),
        in_specs=[pl.BlockSpec(memory_space=pltpu.SMEM)] + [vmem] * 3,
        out_specs=vmem,
        compiler_params=pltpu.CompilerParams(vmem_limit_bytes=14 << 20),
        name="y_far",
    )(core, far, table, part)


def gram_kernel(
    core_ref,
    planes_ref,
    table_ref,
    screens_ref,
    mixed_ref,
    own_ref,
    other_ref,
    coeffs_ref,
    weighted_ref,
    screen_ref,
    sem,
):
    copy = pltpu.make_async_copy(screens_ref, screen_ref, sem)
    copy.start()
    mixed = jnp.concatenate([mixed_ref[...]] * 2, axis=1)
    for b in range(2):
        rows = planes_ref[:, b].reshape(1024, NFIT)
        t0, t1, t2, t3 = [
            jnp.dot(table_ref[256 * t : 256 * t + 256, :], rows, preferred_element_type=F32)
            .astype(BF16)
            .astype(F32)
            for t in range(4)
        ]
        if b == 0:
            copy.wait()
        outs = (t0 - mixed * t3, mixed * t0 + t3, t2 + mixed * t1, mixed * t2 - t1)
        for o, value in enumerate(outs):
            at = slice(256 * o, 256 * o + 256)
            value = value.astype(BF16)
            coeffs_ref[at, 256 * b : 256 * b + 256] = value
            value = value.astype(F32)
            screen = screen_ref[at, :]
            for h in range(2):
                weighted_ref[h, at, 128 * b : 128 * b + 128] = (
                    value[:, 128 * h : 128 * h + 128] * screen
                ).astype(BF16)
    core = core_ref[0]
    for q in range(2):
        left = coeffs_ref[:, 256 * q : 256 * q + 256]
        for half, out_ref in ((core, own_ref), (1 - core, other_ref)):
            got = kernel_scale * lax.dot_general(
                left, weighted_ref[half], (((0,), (0,)), ((), ())), preferred_element_type=F32
            )
            for b in range(2):
                out_ref[32 * q : 32 * q + 32, b] = got[:, 128 * b : 128 * b + 128].reshape(32, 8, 128)


def gram(core, planes, table, screen, mixed):
    half = jax.ShapeDtypeStruct((N, 2, 8, 128), F32)
    return pl.pallas_call(
        gram_kernel,
        out_shape=(half, half),
        in_specs=[pl.BlockSpec(memory_space=pltpu.SMEM)]
        + [pl.BlockSpec(memory_space=pltpu.VMEM)] * 2
        + [pl.BlockSpec(memory_space=pltpu.HBM), pl.BlockSpec(memory_space=pltpu.VMEM)],
        out_specs=[pl.BlockSpec(memory_space=pltpu.VMEM)] * 2,
        scratch_shapes=[
            pltpu.VMEM((1024, 512), BF16),
            pltpu.VMEM((2, 1024, 256), BF16),
            pltpu.VMEM((1024, 128), F32),
            pltpu.SemaphoreType.DMA(()),
        ],
        compiler_params=pltpu.CompilerParams(vmem_limit_bytes=20 << 20),
        name="gram",
    )(core, planes, table, screen, mixed)


def sibling(block):
    return lax.ppermute(block, "c", [(0, 1), (1, 0)])


def exchange(blocks, axes):
    return lax.all_to_all(blocks, axes, split_axis=0, concat_axis=0, tiled=True)


def on_device(orbitals, points):
    core = lax.axis_index("c")
    batch = lax.axis_index("b")
    chip = lax.axis_index(CHIPS)
    core_word = core.astype(jnp.int32)[None]
    y_pair, z_group = chip // 2, core * 4 + chip % 2 * 2 + batch
    base = (chip * 2 + core) * 2048
    place = jnp.stack([core, chip, base]).astype(jnp.int32)
    own, other, ranks, merge_table = pick(place, points, orbitals)
    own = own + sibling(other)
    slots = exchange(jnp.broadcast_to(own[None], (8, CHIP_SLOTS, HALF)), ("z",))

    small = pair_table(iota((N, N), 0), iota((N, N), 1)).astype(BF16)
    z_table, y_big = expand_yz(core_word, small)
    full = (jnp.max(ranks[0]) >= CHIP_SLOTS) | (jnp.max(ranks[1]) >= LINE_SLOTS)
    full = jnp.where(full, F32(1.0), F32(0.0))[None]
    slots, z_table, y_big, full = lax.optimization_barrier((slots, z_table, y_big, full))
    slots = exchange(merge(merge_table, slots), LINES)
    full = full + lax.ppermute(full, "b", [(0, 1), (1, 0)])
    x_small = x_table(y_pair == 0)
    slots, full, x_small, orbitals = lax.optimization_barrier((slots, full, x_small, orbitals))
    own = order(ranks, slots)
    own = lax.cond(
        full[0] > 0,
        lambda o: any_points(points, orbitals, core, base),
        lambda o: o,
        own,
    )
    held = hold(orbitals)
    near, far = fit(core_word, own, sibling(own), z_table, held)
    x_big = expand_x(x_small)
    screen, mixed = screen_rows(y_pair, z_group * 4)
    screen = pltpu.with_memory_space_constraint(screen, pltpu.HBM)
    planes = y_far(core_word, sibling(far), y_big, y_near(core_word, near, y_big))
    planes = exchange(planes.reshape(128, 16, NFIT), SAME_CORE).reshape(N, 2, 16, NFIT)
    own, other = gram(core_word, planes, x_big, screen, mixed)
    sums = exchange((own + sibling(other)).reshape(128, 8, 128), SAME_CORE)
    sums = jnp.sum(sums, axis=0).reshape(2, 4, 128)
    mine = lax.dynamic_index_in_dim(sums, core, 0, keepdims=False)
    theirs = sibling(lax.dynamic_index_in_dim(sums, 1 - core, 0, keepdims=False))
    pair = jnp.where(core == 0, jnp.stack([mine, theirs]), jnp.stack([theirs, mine]))
    return pair.transpose(0, 2, 1).reshape(NFIT, 4)


def solution(mesh):
    fine = Mesh(mesh.devices.reshape(2, 4, 8, 2, 2), ("yl", "x", "z", "c", "b"))
    grid = ("yl", "x", "z", "c")
    return jax.shard_map(
        on_device,
        mesh=fine,
        in_specs=(P(None, grid), P("b", None)),
        out_specs=P("b", grid),
        check_vma=False,
    )
```

```python
import math

import jax
import jax.numpy as jnp
from jax import lax
from jax.experimental import pallas as pl
from jax.experimental.pallas import tpu as pltpu
from jax.sharding import Mesh
from jax.sharding import PartitionSpec as P

N = 64
NORB = 1024
NFIT = 256
HALF = NORB // 2
CHIP_SLOTS = 16
LINE_SLOTS = 64

screen_rate = 0.05
kernel_scale = 16.0

CHIPS = ("yl", "x", "z")
LINES = ("yl", "x")
SAME_CORE = ("yl", "x", "z", "b")
F32 = jnp.float32
BF16 = jnp.bfloat16


def signed_freq(values):
    return jnp.where(values < N // 2, values, values - N).astype(F32)


def waves(freq, place):
    angles = (freq * place % N).astype(F32) * F32(2.0 * math.pi / N)
    return jnp.cos(angles) / math.sqrt(N), jnp.sin(angles) / math.sqrt(N)


def iota(shape, dim):
    return lax.broadcasted_iota(jnp.int32, shape, dim)


def pair_table(row, place):
    pair, part = row // 2, row % 2
    freq = jnp.where((pair == 0) & (part == 1), N // 2, pair)
    cosine, sine = waves(freq, place)
    return jnp.where((part == 0) | (pair == 0), cosine, -sine)


def x_table(lone):
    row, column = iota((256, 256), 0), iota((256, 256), 1)
    z_of, e, k = row // 128, row // 64 % 2, row % 64
    z_part, y_part, place = column // 128, column // 64 % 2, column % 64
    k_low = k % 32
    turned = (e == 1) & (k_low == 0)
    freq = jnp.where(lone, jnp.where(turned, N // 2, k_low), k)
    cosine, sine = waves(freq, place)
    both = jnp.where(e == y_part, cosine, jnp.where(e == 0, sine, -sine))
    both = jnp.where(z_of == z_part, both, F32(0.0))
    single = jnp.where((e == 0) | turned, cosine, -sine)
    kept = (y_part == k // 32) & (z_part == jnp.where(turned, 1 - z_of, z_of))
    return jnp.where(lone, jnp.where(kept, single, F32(0.0)), both).astype(BF16)


def screen_rows(y_pair, z_first):
    shape = (1024, 128)
    row = iota(shape, 0)
    out, k, z_pair = row // 256, row // 4 % 64, z_first + row % 4
    lone_y, lone_z = y_pair == 0, z_pair == 0
    k_low = k % 32
    edge = lone_y & (k_low == 0)
    second = (out == 1) | (out == 3)
    kx = jnp.where(lone_y, jnp.where(edge & second, N // 2, k_low), k)
    ky = jnp.where(lone_y, jnp.where(k >= 32, N // 2, 0), y_pair)
    z_late = (out == 2) | jnp.where(edge, out == 3, out == 1)
    kz = jnp.where(lone_z, jnp.where(z_late, N // 2, 0), z_pair)
    fx, fy, fz = signed_freq(kx), signed_freq(ky), signed_freq(kz)
    scaled = screen_rate * (fx * fx + fy * fy + fz * fz)
    positive = scaled > 0
    safe = jnp.where(positive, scaled, F32(1.0))
    screen = jnp.where(positive, -jnp.expm1(-safe) / safe, F32(0.0))
    copies = jnp.where(edge & lone_z, F32(1.0), F32(2.0))
    mixed = jnp.where(lone_z | edge, F32(0.0), F32(1.0))[:256]
    return screen * copies, mixed


def spread(small, row_of, column_of, first, rows, columns):
    r = first + iota((rows, small.shape[0]), 0)
    c = iota((small.shape[1], columns), 1)
    left = jnp.where(row_of(r) == iota(r.shape, 1), F32(1.0), F32(0.0)).astype(BF16)
    right = jnp.where(column_of(c) == iota(c.shape, 0), F32(1.0), F32(0.0)).astype(BF16)
    tall = jnp.dot(left, small, preferred_element_type=F32).astype(BF16)
    return jnp.dot(tall, right, preferred_element_type=F32)


def expand_yz_kernel(core_ref, small_ref, z_ref, y_ref):
    core = core_ref[0]
    small = small_ref[...]
    row, column = iota((256, 256), 0), iota((256, 256), 1)
    wide = spread(
        small,
        lambda r: jnp.where(r < 128, core, 1 - core) * 32 + (r & 31),
        lambda c: c & 63,
        0,
        256,
        256,
    )
    same = ((row >> 5) & 3) == (column >> 6)
    z_ref[...] = jnp.where(same, wide, F32(0.0)).astype(BF16)
    column = iota((256, 1024), 1)
    for block in range(4):
        row = 256 * block + iota((256, 1024), 0)
        wide = spread(
            small, lambda r: (r >> 5) * 2 + ((r >> 3) & 1), lambda c: c >> 4, 256 * block, 256, 1024
        )
        same = (((row >> 4) & 1) == ((column >> 3) & 1)) & ((row & 7) == (column & 7))
        y_ref[256 * block : 256 * block + 256, :] = jnp.where(same, wide, F32(0.0)).astype(BF16)


def expand_yz(core, small):
    vmem = pl.BlockSpec(memory_space=pltpu.VMEM)
    return pl.pallas_call(
        expand_yz_kernel,
        out_shape=(
            jax.ShapeDtypeStruct((256, 256), BF16),
            jax.ShapeDtypeStruct((1024, 1024), BF16),
        ),
        in_specs=[pl.BlockSpec(memory_space=pltpu.SMEM), vmem],
        out_specs=[vmem] * 2,
        compiler_params=pltpu.CompilerParams(vmem_limit_bytes=16 << 20),
        cost_estimate=pl.CostEstimate(flops=2**30, bytes_accessed=2**21, transcendentals=0),
        name="expand_yz",
    )(core, small)


def expand_x_kernel(small_ref, x_ref):
    column = iota((256, 1024), 1)
    for block in range(4):
        row = 256 * block + iota((256, 1024), 0)
        wide = spread(
            small_ref[...],
            lambda r: r >> 2,
            lambda c: (c & 1) * 128 + ((c >> 3) & 1) * 64 + (c >> 4),
            256 * block,
            256,
            1024,
        )
        same = (row & 3) == ((column >> 1) & 3)
        x_ref[256 * block : 256 * block + 256, :] = jnp.where(same, wide, F32(0.0)).astype(BF16)


def expand_x(small):
    vmem = pl.BlockSpec(memory_space=pltpu.VMEM)
    return pl.pallas_call(
        expand_x_kernel,
        out_shape=jax.ShapeDtypeStruct((1024, 1024), BF16),
        in_specs=[vmem],
        out_specs=vmem,
        compiler_params=pltpu.CompilerParams(vmem_limit_bytes=16 << 20),
        cost_estimate=pl.CostEstimate(flops=2**31, bytes_accessed=2**21, transcendentals=0),
        name="expand_x",
    )(small)


def pick_kernel(
    place_ref, points_ref, orbitals_ref, own_ref, other_ref, ranks_ref, merge_ref, held_ref, got_ref, sem
):
    copy = pltpu.make_async_copy(orbitals_ref, held_ref, sem)
    copy.start()
    core, chip, base = place_ref[0], place_ref[1], place_ref[2]
    points = points_ref[...]
    columns = jnp.broadcast_to(points.astype(F32), (128, NFIT)).T.astype(jnp.int32)
    column = jnp.concatenate([columns] * 2, axis=1)
    before_row = iota((NFIT, NFIT), 0) < iota((NFIT, NFIT), 1)
    before_column = iota((NFIT, NFIT), 1) < iota((NFIT, NFIT), 0)

    def count(matches, axis):
        return jnp.sum(jnp.where(matches, F32(1.0), F32(0.0)), axis=axis, keepdims=True)

    same_chip = (column >> 12) == (points >> 12)
    same_line = (column >> 15) == (points >> 15)
    chip_rank = count(same_chip & before_row, 0).astype(jnp.int32)
    line_rank = count(same_line & before_row, 0).astype(jnp.int32)
    rank_column = count(same_chip & before_column, 1).astype(jnp.int32)
    ranks_ref[0:1, :] = chip_rank
    ranks_ref[1:2, :] = line_rank
    ranks_ref[2:3, :] = points >> 15

    slot = iota((NFIT, 128), 1)
    chosen = ((columns >> 12) == chip) & (rank_column == slot)
    offsets = jnp.max(
        jnp.where(chosen, (columns - base).astype(F32), F32(-1.0)), axis=0, keepdims=True
    ).astype(jnp.int32)
    hot = jnp.where(iota((2048, 128), 0) == offsets, F32(1.0), F32(0.0)).astype(BF16)

    to_slot = ((points >> 15) == (chip >> 3)) & (line_rank == iota((LINE_SLOTS, NFIT), 0))
    from_slot = (((columns >> 12) & 7) == (slot >> 4)) & (rank_column == (slot & 15))
    merge_ref[...] = jnp.dot(
        jnp.where(to_slot, F32(1.0), F32(0.0)).astype(BF16),
        jnp.where(from_slot, F32(1.0), F32(0.0)).astype(BF16),
        preferred_element_type=F32,
    ).astype(BF16)

    copy.wait()
    got = jnp.dot(held_ref[...], hot, preferred_element_type=F32)
    got_ref[...] = got.T[:CHIP_SLOTS].astype(BF16)
    own_ref[...] = got_ref[:, pl.ds(pl.multiple_of(core * HALF, HALF), HALF)]
    other_ref[...] = got_ref[:, pl.ds(pl.multiple_of((1 - core) * HALF, HALF), HALF)]


def pick(place, points, orbitals):
    half = jax.ShapeDtypeStruct((CHIP_SLOTS, HALF), BF16)
    vmem = pl.BlockSpec(memory_space=pltpu.VMEM)
    return pl.pallas_call(
        pick_kernel,
        out_shape=(
            half,
            half,
            jax.ShapeDtypeStruct((8, NFIT), jnp.int32),
            jax.ShapeDtypeStruct((LINE_SLOTS, 128), BF16),
        ),
        in_specs=[pl.BlockSpec(memory_space=pltpu.SMEM), vmem, pl.BlockSpec(memory_space=pltpu.HBM)],
        out_specs=[vmem] * 4,
        scratch_shapes=[
            pltpu.VMEM((NORB, 2048), BF16),
            pltpu.VMEM((CHIP_SLOTS, NORB), BF16),
            pltpu.SemaphoreType.DMA(()),
        ],
        compiler_params=pltpu.CompilerParams(vmem_limit_bytes=16 << 20),
        name="pick",
    )(place, points, orbitals)


def merge_kernel(merge_ref, slots_ref, out_ref):
    got = jnp.dot(
        merge_ref[...], slots_ref[...].reshape(128, HALF), preferred_element_type=F32
    ).astype(BF16)
    for i in range(8):
        out_ref[i] = got


def merge(table, slots):
    vmem = pl.BlockSpec(memory_space=pltpu.VMEM)
    return pl.pallas_call(
        merge_kernel,
        out_shape=jax.ShapeDtypeStruct((8, LINE_SLOTS, HALF), BF16),
        in_specs=[vmem] * 2,
        out_specs=vmem,
        compiler_params=pltpu.CompilerParams(vmem_limit_bytes=8 << 20),
        name="merge",
    )(table, slots)


def order_kernel(ranks_ref, slots_ref, out_ref):
    row = iota((8 * LINE_SLOTS, NFIT), 0)
    here = ((row >> 6) == ranks_ref[2:3, :]) & ((row & 63) == ranks_ref[1:2, :])
    out_ref[...] = lax.dot_general(
        slots_ref[...].reshape(8 * LINE_SLOTS, HALF),
        jnp.where(here, F32(1.0), F32(0.0)).astype(BF16),
        (((0,), (0,)), ((), ())),
        preferred_element_type=F32,
    ).astype(BF16)


def order(ranks, slots):
    vmem = pl.BlockSpec(memory_space=pltpu.VMEM)
    return pl.pallas_call(
        order_kernel,
        out_shape=jax.ShapeDtypeStruct((HALF, NFIT), BF16),
        in_specs=[vmem] * 2,
        out_specs=vmem,
        compiler_params=pltpu.CompilerParams(vmem_limit_bytes=8 << 20),
        name="order",
    )(ranks, slots)


def any_points(points, orbitals, core, base):
    cell = iota((2048, NFIT), 0) + base
    hot = jnp.where(cell == points, F32(1.0), F32(0.0)).astype(BF16)
    got = jnp.dot(orbitals, hot, preferred_element_type=F32).astype(BF16)
    own = lax.dynamic_slice_in_dim(got, core * HALF, HALF, 0)
    other = lax.dynamic_slice_in_dim(got, (1 - core) * HALF, HALF, 0)
    own = exchange((own + sibling(other)).reshape(N, 8, NFIT), CHIPS)
    own = jnp.sum(own.astype(F32), axis=0).astype(BF16)
    return exchange(jnp.broadcast_to(own[None], (N, 8, NFIT)), CHIPS).reshape(HALF, NFIT)


def hold_kernel(orbitals_ref, held_ref, sem):
    copy = pltpu.make_async_copy(orbitals_ref, held_ref, sem)
    copy.start()
    copy.wait()


def hold(orbitals):
    return pl.pallas_call(
        hold_kernel,
        out_shape=jax.ShapeDtypeStruct(orbitals.shape, orbitals.dtype),
        in_specs=[pl.BlockSpec(memory_space=pltpu.HBM)],
        out_specs=pl.BlockSpec(memory_space=pltpu.VMEM),
        scratch_shapes=[pltpu.SemaphoreType.DMA(())],
        compiler_params=pltpu.CompilerParams(vmem_limit_bytes=8 << 20),
        cost_estimate=pl.CostEstimate(flops=0, bytes_accessed=2**23, transcendentals=0),
        name="hold",
    )(orbitals)


def fit_kernel(core_ref, own_ref, other_ref, table_ref, orbitals_ref, near_ref, far_ref, values_ref):
    core = core_ref[0]
    mine = pl.multiple_of(core * HALF, HALF)
    theirs = pl.multiple_of((1 - core) * HALF, HALF)
    values_ref[pl.ds(mine, HALF), :] = own_ref[...]
    values_ref[pl.ds(theirs, HALF), :] = other_ref[...]
    density = lax.dot_general(
        orbitals_ref[...], values_ref[...], (((0,), (0,)), ((), ())), preferred_element_type=F32
    )
    fitted = (density * density).astype(BF16)
    for j in range(8):
        half_z = jnp.dot(
            table_ref[...], fitted[256 * j : 256 * j + 256], preferred_element_type=F32
        ).astype(BF16)
        near_ref[4 * j : 4 * j + 4] = half_z[:128].reshape(4, 32, NFIT)
        far_ref[4 * j : 4 * j + 4] = half_z[128:].reshape(4, 32, NFIT)


def fit(core, own, other, table, held):
    half = jax.ShapeDtypeStruct((32, 32, NFIT), BF16)
    vmem = pl.BlockSpec(memory_space=pltpu.VMEM)
    return pl.pallas_call(
        fit_kernel,
        out_shape=(half, half),
        in_specs=[pl.BlockSpec(memory_space=pltpu.SMEM)] + [vmem] * 4,
        out_specs=[vmem] * 2,
        scratch_shapes=[pltpu.VMEM((NORB, NFIT), BF16)],
        compiler_params=pltpu.CompilerParams(vmem_limit_bytes=16 << 20),
        name="fit",
    )(core, own, other, table, held)


def y_near_kernel(core_ref, near_ref, table_ref, part_ref):
    at = pl.ds(pl.multiple_of(core_ref[0] * 512, 512), 512)
    for g in range(2):
        rows = near_ref[:, 16 * g : 16 * g + 16, :].reshape(512, NFIT)
        part_ref[g] = jnp.dot(table_ref[:, at], rows, preferred_element_type=F32)


def y_near(core, near, table):
    vmem = pl.BlockSpec(memory_space=pltpu.VMEM)
    return pl.pallas_call(
        y_near_kernel,
        out_shape=jax.ShapeDtypeStruct((2, 1024, NFIT), F32),
        in_specs=[pl.BlockSpec(memory_space=pltpu.SMEM)] + [vmem] * 2,
        out_specs=vmem,
        compiler_params=pltpu.CompilerParams(vmem_limit_bytes=12 << 20),
        cost_estimate=pl.CostEstimate(flops=2**29, bytes_accessed=2**22, transcendentals=0),
        name="y_near",
    )(core, near, table)


def y_far_kernel(core_ref, far_ref, table_ref, part_ref, out_ref):
    at = pl.ds(pl.multiple_of((1 - core_ref[0]) * 512, 512), 512)
    for g in range(2):
        rows = far_ref[:, 16 * g : 16 * g + 16, :].reshape(512, NFIT)
        got = part_ref[g] + jnp.dot(table_ref[:, at], rows, preferred_element_type=F32)
        out_ref[:, g] = got.astype(BF16).reshape(32, 2, 16, NFIT)


def y_far(core, far, table, part):
    vmem = pl.BlockSpec(memory_space=pltpu.VMEM)
    return pl.pallas_call(
        y_far_kernel,
        out_shape=jax.ShapeDtypeStruct((32, 2, 2, 16, NFIT), BF16),
        in_specs=[pl.BlockSpec(memory_space=pltpu.SMEM)] + [vmem] * 3,
        out_specs=vmem,
        compiler_params=pltpu.CompilerParams(vmem_limit_bytes=14 << 20),
        name="y_far",
    )(core, far, table, part)


def gram_kernel(
    core_ref,
    planes_ref,
    table_ref,
    screens_ref,
    mixed_ref,
    own_ref,
    other_ref,
    coeffs_ref,
    weighted_ref,
    screen_ref,
    sem,
):
    copy = pltpu.make_async_copy(screens_ref, screen_ref, sem)
    copy.start()
    mixed = jnp.concatenate([mixed_ref[...]] * 2, axis=1)
    for b in range(2):
        rows = planes_ref[:, b].reshape(1024, NFIT)
        t0, t1, t2, t3 = [
            jnp.dot(table_ref[256 * t : 256 * t + 256, :], rows, preferred_element_type=F32)
            .astype(BF16)
            .astype(F32)
            for t in range(4)
        ]
        if b == 0:
            copy.wait()
        outs = (t0 - mixed * t3, mixed * t0 + t3, t2 + mixed * t1, mixed * t2 - t1)
        for o, value in enumerate(outs):
            at = slice(256 * o, 256 * o + 256)
            value = value.astype(BF16)
            coeffs_ref[at, 256 * b : 256 * b + 256] = value
            value = value.astype(F32)
            screen = screen_ref[at, :]
            for h in range(2):
                weighted_ref[h, at, 128 * b : 128 * b + 128] = (
                    value[:, 128 * h : 128 * h + 128] * screen
                ).astype(BF16)
    core = core_ref[0]
    for q in range(2):
        left = coeffs_ref[:, 256 * q : 256 * q + 256]
        for half, out_ref in ((core, own_ref), (1 - core, other_ref)):
            got = kernel_scale * lax.dot_general(
                left, weighted_ref[half], (((0,), (0,)), ((), ())), preferred_element_type=F32
            )
            for b in range(2):
                out_ref[32 * q : 32 * q + 32, b] = got[:, 128 * b : 128 * b + 128].reshape(32, 8, 128)


def gram(core, planes, table, screen, mixed):
    half = jax.ShapeDtypeStruct((N, 2, 8, 128), F32)
    return pl.pallas_call(
        gram_kernel,
        out_shape=(half, half),
        in_specs=[pl.BlockSpec(memory_space=pltpu.SMEM)]
        + [pl.BlockSpec(memory_space=pltpu.VMEM)] * 2
        + [pl.BlockSpec(memory_space=pltpu.HBM), pl.BlockSpec(memory_space=pltpu.VMEM)],
        out_specs=[pl.BlockSpec(memory_space=pltpu.VMEM)] * 2,
        scratch_shapes=[
            pltpu.VMEM((1024, 512), BF16),
            pltpu.VMEM((2, 1024, 256), BF16),
            pltpu.VMEM((1024, 128), F32),
            pltpu.SemaphoreType.DMA(()),
        ],
        compiler_params=pltpu.CompilerParams(vmem_limit_bytes=20 << 20),
        name="gram",
    )(core, planes, table, screen, mixed)


def sibling(block):
    return lax.ppermute(block, "c", [(0, 1), (1, 0)])


def exchange(blocks, axes):
    return lax.all_to_all(blocks, axes, split_axis=0, concat_axis=0, tiled=True)


def on_device(orbitals, points):
    core = lax.axis_index("c")
    batch = lax.axis_index("b")
    chip = lax.axis_index(CHIPS)
    core_word = core.astype(jnp.int32)[None]
    y_pair, z_group = chip // 2, core * 4 + chip % 2 * 2 + batch
    base = (chip * 2 + core) * 2048
    place = jnp.stack([core, chip, base]).astype(jnp.int32)
    own, other, ranks, merge_table = pick(place, points, orbitals)
    own = own + sibling(other)
    slots = exchange(jnp.broadcast_to(own[None], (8, CHIP_SLOTS, HALF)), ("z",))

    small = pair_table(iota((N, N), 0), iota((N, N), 1)).astype(BF16)
    z_table, y_big = expand_yz(core_word, small)
    full = (jnp.max(ranks[0]) >= CHIP_SLOTS) | (jnp.max(ranks[1]) >= LINE_SLOTS)
    full = jnp.where(full, F32(1.0), F32(0.0))[None]
    slots, z_table, y_big, full = lax.optimization_barrier((slots, z_table, y_big, full))
    slots = exchange(merge(merge_table, slots), LINES)
    full = full + lax.ppermute(full, "b", [(0, 1), (1, 0)])
    slots, full, orbitals = lax.optimization_barrier((slots, full, orbitals))
    own = order(ranks, slots)
    own = lax.cond(
        full[0] > 0,
        lambda o: any_points(points, orbitals, core, base),
        lambda o: o,
        own,
    )
    held = hold(orbitals)
    near, far = fit(core_word, own, sibling(own), z_table, held)
    x_big = expand_x(x_table(y_pair == 0))
    screen, mixed = screen_rows(y_pair, z_group * 4)
    screen = pltpu.with_memory_space_constraint(screen, pltpu.HBM)
    planes = y_far(core_word, sibling(far), y_big, y_near(core_word, near, y_big))
    planes = exchange(planes.reshape(128, 16, NFIT), SAME_CORE).reshape(N, 2, 16, NFIT)
    own, other = gram(core_word, planes, x_big, screen, mixed)
    sums = exchange((own + sibling(other)).reshape(128, 8, 128), SAME_CORE)
    sums = jnp.sum(sums, axis=0).reshape(2, 4, 128)
    mine = lax.dynamic_index_in_dim(sums, core, 0, keepdims=False)
    theirs = sibling(lax.dynamic_index_in_dim(sums, 1 - core, 0, keepdims=False))
    pair = jnp.where(core == 0, jnp.stack([mine, theirs]), jnp.stack([theirs, mine]))
    return pair.transpose(0, 2, 1).reshape(NFIT, 4)


def solution(mesh):
    fine = Mesh(mesh.devices.reshape(2, 4, 8, 2, 2), ("yl", "x", "z", "c", "b"))
    grid = ("yl", "x", "z", "c")
    return jax.shard_map(
        on_device,
        mesh=fine,
        in_specs=(P(None, grid), P("b", None)),
        out_specs=P("b", grid),
        check_vma=False,
    )
```
